256 devices in a mesh: ctx: 32 (over z, y), head: 8 (over x, core).
Axes of the slice: x: 4, y: 4, z: 8, core: 2. Of those that a mesh axis runs over, the one named last changes fastest.
Arguments:
- tokens: bfloat16 [16384, 2048], P('ctx'), may hold values from -6 to 6
- w_proj: bfloat16 [2048, 10240], P('ctx', 'head'), may hold values from -0.125 to 0.125
- w_small: bfloat16 [2048, 48], P('ctx', 'head'), may hold values from -0.125 to 0.125
- beta_bias: float32 [16, 2], P('head'), may hold values from 5 to 9
- decay_rate: float32 [16], P('head'), may hold values from 5e-07 to 0.05
- w_out: bfloat16 [2048, 2048], P('head', 'ctx'), may hold values from -0.125 to 0.125
Outputs:
- mixed: bfloat16 [16384, 2048], P(('ctx', 'head'))
The draws below stay inside these ranges and needn't reach their ends.
All inputs are finite; a program needn't handle non-finite values.
Results may differ from the reference program's by a relative error of at most 0.006.
Values may be sent and summed in bfloat16 or wider, within the bound.
No kernel may reach another device: no remote copies, remote signals or barrier semaphores. Data moves between devices by JAX's collectives and lax.ppermute only.
A program may use at most 128 MiB of HBM per device.

```python
import math
import jax
import jax.numpy as jnp
from jax import lax

D = 2048
HEADS = 16
DK = 128
REFLECTIONS = 2
TOKENS = 16384


def draw_decay_rate(key, part):
    uniform_part = jax.random.uniform(key, (HEADS,), jnp.float32)
    lowest = math.log(5e-07)
    upper_end = math.log(0.05)
    return jnp.exp(lowest + uniform_part * (upper_end - lowest))


def steps_of(own_key, dims, pieces, low, top_value):
    loudness = 1.0
    for axis_at, shards_of in pieces:
        heights = jax.random.uniform(jax.random.fold_in(jax.random.fold_in(own_key, 6), axis_at), (shards_of,), jnp.float32, low / len(pieces), top_value / len(pieces))
        loudness = loudness * jnp.repeat(jnp.exp(heights), dims[axis_at] // shards_of).reshape((-1,) + (1,) * (len(dims) - 1 - axis_at))
    return loudness


def noise(key, dims, spread, most, cuts=(), dtype=jnp.bfloat16):
    result = spread * jax.random.normal(key, dims, jnp.float32)
    if cuts:
        result = result * steps_of(key, dims, cuts, -0.22, 0.18)
    return jnp.clip(result, -most, most).astype(dtype)


def setup_inputs(seed: int = 0) -> dict:
    splits = jax.random.split(jax.random.key(seed), 7)
    return {
        "tokens": noise(splits[0], (TOKENS, D), 1.0, 6.0, ((0, 32),)),
        "w_proj": noise(splits[1], (D, HEADS * (1 + 2 * REFLECTIONS) * DK), D ** -0.5, 0.125, ((0, 32), (1, 8))),
        "w_small": noise(splits[2], (D, HEADS * (REFLECTIONS + 1)), D ** -0.5, 0.125, ((0, 32), (1, 8))),
        "beta_bias": jnp.clip(5.0 + 4.0 * jax.random.uniform(splits[3], (HEADS, REFLECTIONS), jnp.float32) ** steps_of(splits[3], (HEADS, REFLECTIONS), ((0, 8),), -0.2, 0.2), 5.0, 9.0),
        "decay_rate": draw_decay_rate(jax.random.fold_in(splits[6], 71), 0),
        "w_out": noise(splits[5], (HEADS * DK, D), (HEADS * DK) ** -0.5, 0.125, ((0, 8), (1, 32))),
    }


HIGHEST_PRECISION = lax.Precision.HIGHEST

def unit_rows(vectors):
    return vectors / jnp.sqrt(lax.optimization_barrier(jnp.sum(vectors * vectors, axis=-1, keepdims=True)) + 1e-06)

def reference(tokens, w_proj, w_small, beta_bias, decay_rate, w_out):
    block_rows = math.gcd(TOKENS, 256)
    blocks = TOKENS // block_rows
    mirrors = REFLECTIONS

    def token_step(state, inputs):
        query, keys, values, betas, decay = inputs
        state = decay[:, None, None] * state
        for index in range(mirrors):
            key_now = keys[:, index]
            recalled = jnp.einsum('hab,hb->ha', state, key_now, precision=HIGHEST_PRECISION)
            change = (values[:, index] - recalled) * betas[:, index, None]
            state = state + change[:, :, None] * key_now[:, None, :]
        return (state, jnp.einsum('hab,hb->ha', state, query, precision=HIGHEST_PRECISION))

    def block_step(state, rows):
        projected = jnp.dot(rows, w_proj, preferred_element_type=jnp.float32)
        gate_inputs = jnp.dot(rows, w_small, preferred_element_type=jnp.float32)
        parts = projected.reshape(block_rows, HEADS, 1 + 2 * mirrors, DK)
        queries = unit_rows(parts[:, :, 0])
        keys_all = unit_rows(parts[:, :, 1:1 + mirrors])
        values_all = parts[:, :, 1 + mirrors:]
        gate_cols = gate_inputs.reshape(block_rows, HEADS, mirrors + 1)
        betas = 2.0 * jax.nn.sigmoid(gate_cols[:, :, :mirrors] + beta_bias[None])
        decay = jnp.exp(-decay_rate[None, :] * jax.nn.softplus(gate_cols[:, :, mirrors]))
        state, head_out = lax.scan(token_step, state, (queries, keys_all, values_all, betas, decay))
        normed = head_out / jnp.sqrt(lax.optimization_barrier(jnp.mean(head_out * head_out, axis=-1, keepdims=True)) + 1e-06)
        normed = normed.astype(jnp.bfloat16).reshape(block_rows, HEADS * DK)
        return (state, jnp.dot(normed, w_out, preferred_element_type=jnp.float32).astype(jnp.bfloat16))
    start = jnp.zeros((HEADS, DK, DK), jnp.float32)
    final_state, mixed = lax.scan(block_step, start, tokens.reshape(blocks, block_rows, D))
    return mixed.reshape(TOKENS, D)
```

```python
import functools

import jax
import jax.numpy as jnp
from jax import lax
from jax.experimental import pallas as pl
from jax.experimental.pallas import tpu as pltpu
from jax.sharding import PartitionSpec as P

F32 = jnp.float32
BF16 = jnp.bfloat16
LANES = 128
BLOCK = 64
ROWS = (((1,), (0,)), ((), ()))
NT = (((1,), (1,)), ((), ()))
TN = (((0,), (0,)), ((), ()))


def split(array):
    high = array.astype(BF16)
    return high, (array - high.astype(F32)).astype(BF16)


def dot1(left, right, dims):
    return lax.dot_general(left, right, dims, preferred_element_type=F32)


def dot3(left, right, dims):
    return (
        dot1(left[0], right[0], dims)
        + dot1(left[0], right[1], dims)
        + dot1(left[1], right[0], dims)
    )


def shift(array, by):
    count = lax.axis_size("ctx")
    return lax.ppermute(array, "ctx", [(i, i + by) for i in range(count - by)])


def around(array, y_size, dz, dy):
    count = lax.axis_size("ctx")
    z_size = count // y_size
    pairs = [
        (z * y_size + y, ((z + dz) % z_size) * y_size + (y + dy) % y_size)
        for z in range(z_size)
        for y in range(y_size)
    ]
    return lax.ppermute(array, "ctx", pairs)


def unit(rows):
    return rows / jnp.sqrt(jnp.sum(rows * rows, axis=-1, keepdims=True) + 1e-06)


def local_kernel(head, proj_ref, gate_ref, row_ref, state_ref, query_ref, out_ref):
    tokens = proj_ref.shape[0]
    width = LANES
    blocks = tokens // BLOCK
    span = 2 * BLOCK
    gates = gate_ref[...]
    bias = row_ref[0:1, :]
    rate = row_ref[1:2, :]
    betas = 2.0 / (1.0 + jnp.exp(-(gates + bias)))
    soft = jnp.maximum(gates, 0.0) + jnp.log1p(jnp.exp(-jnp.abs(gates)))
    log_decay = -rate * soft
    row64 = lax.broadcasted_iota(jnp.int32, (BLOCK, BLOCK), 0)
    col64 = lax.broadcasted_iota(jnp.int32, (BLOCK, BLOCK), 1)
    lower = jnp.where(row64 >= col64, 1.0, 0.0).astype(F32)
    base = 3 * head
    row_i = lax.broadcasted_iota(jnp.int32, (span, span), 0)
    col_i = lax.broadcasted_iota(jnp.int32, (span, span), 1)
    row_t, row_r = row_i % BLOCK, row_i // BLOCK
    col_t, col_r = col_i % BLOCK, col_i // BLOCK
    strict = (row_t > col_t) | ((row_t == col_t) & (row_r > col_r))
    within = (row_t == col_t) & (row_r > col_r)
    eye = jnp.where(row_i == col_i, 1.0, 0.0).astype(F32)
    visible = (
        lax.broadcasted_iota(jnp.int32, (BLOCK, span), 0)
        >= lax.broadcasted_iota(jnp.int32, (BLOCK, span), 1) % BLOCK
    )
    levels = []
    size = 1
    while size < BLOCK:
        levels.append(
            (row_t // (2 * size) == col_t // (2 * size))
            & ((row_t // size) % 2 == 1)
            & ((col_t // size) % 2 == 0)
        )
        size *= 2

    def prepare(n):
        rows = slice(n * BLOCK, (n + 1) * BLOCK)
        query = unit(proj_ref[rows, 0:width])
        keys = jnp.concatenate(
            [
                unit(proj_ref[rows, width : 2 * width]),
                unit(proj_ref[rows, 2 * width : 3 * width]),
            ],
            axis=0,
        )
        values = jnp.concatenate(
            [proj_ref[rows, 3 * width : 4 * width], proj_ref[rows, 4 * width : 5 * width]], axis=0
        )
        beta = jnp.concatenate(
            [betas[rows, base : base + 1], betas[rows, base + 1 : base + 2]], axis=0
        )
        running = jnp.dot(
            lower, log_decay[rows], precision=lax.Precision.HIGHEST, preferred_element_type=F32
        )
        across = jnp.transpose(running)[base + 2 : base + 3, :]
        down = running[:, base + 2 : base + 3]
        across = jnp.concatenate([across, across], axis=1)
        reach = jnp.exp(jnp.where(visible, down - across, 0.0))
        keys_s = split(keys)
        both = jnp.concatenate([query, keys], axis=0)
        scores = dot3(split(both), keys_s, NT)
        attend = jnp.where(visible, reach, 0.0) * scores[:BLOCK]
        system = jnp.where(
            strict, beta * jnp.concatenate([reach, reach], axis=0) * scores[BLOCK:], 0.0
        )
        grow = jnp.exp(down)
        grow2 = jnp.concatenate([grow, grow], axis=0)
        last = running[BLOCK - 1 : BLOCK, base + 2 : base + 3]
        tail = jnp.exp(last - down)
        tail2 = jnp.concatenate([tail, tail], axis=0)
        right = jnp.concatenate([beta * grow2 * keys, beta * values], axis=1)
        return dict(
            query=query * grow,
            keys=keys_s,
            attend=attend,
            system=system,
            right=right,
            tail=tail2,
            last=jnp.exp(last),
            inverse=eye - jnp.where(within, system, 0.0),
        )

    parts = [prepare(n) for n in range(blocks)]
    for level in levels:
        for part in parts:
            inverse = split(part["inverse"])
            corner = split(jnp.where(level, part["system"], 0.0))
            middle = dot3(corner, inverse, ROWS)
            part["inverse"] = part["inverse"] - dot3(inverse, split(middle), ROWS)
    for part in parts:
        solved = dot3(split(part["inverse"]), split(part["right"]), ROWS)
        part["step"] = dot3(split(solved * part["tail"]), part["keys"], TN)
        seen = dot3(split(part["attend"]), split(solved), ROWS)
        part["query"] = part["query"] - seen[:, :width]
        part["seen"] = seen[:, width:]
    zero = jnp.zeros((width, width), F32)
    state = jnp.concatenate([eye, zero], axis=0)
    for n, part in enumerate(parts):
        rows = slice(n * BLOCK, (n + 1) * BLOCK)
        state_s = split(state)
        reads = dot3(split(part["query"]), state_s, NT)
        query_ref[rows, :] = reads[:, :width]
        out_ref[rows, :] = reads[:, width:] + part["seen"]
        move = part["last"] * eye - part["step"][:width]
        state = dot3(state_s, split(move), ROWS)
        state = state + jnp.concatenate([zero, part["step"][width:]], axis=0)
    state_ref[...] = state


def local_pass(proj, gates, rows, head):
    tokens = proj.shape[0]
    whole = lambda: (0, 0)
    return pl.pallas_call(
        functools.partial(local_kernel, head),
        out_shape=(
            jax.ShapeDtypeStruct((2 * LANES, LANES), F32),
            jax.ShapeDtypeStruct((tokens, LANES), F32),
            jax.ShapeDtypeStruct((tokens, LANES), F32),
        ),
        name=f"local{head}",
    )(proj, gates, rows)


def finish_kernel(state_ref, query_ref, part_ref, out_ref):
    heads = state_ref.shape[0]
    for head in range(heads):
        total = part_ref[head] + dot3(split(query_ref[head]), split(state_ref[head]), NT)
        scale = jnp.sqrt(jnp.mean(total * total, axis=-1, keepdims=True) + 1e-06)
        out_ref[:, head * LANES : (head + 1) * LANES] = (total / scale).astype(BF16)


def compose_kernel(before_ref, now_ref, out_ref):
    for head in range(now_ref.shape[0]):
        now = now_ref[head]
        moved = dot3(
            split(before_ref[head].astype(F32)), split(now[:LANES].astype(F32)), ROWS
        )
        rows = before_ref.shape[1]
        if rows > LANES:
            out_ref[head, : rows - LANES] = moved[: rows - LANES]
        out_ref[head, rows - LANES :] = moved[rows - LANES :] + now[LANES:].astype(F32)


def compose(before, now):
    return pl.pallas_call(
        compose_kernel,
        out_shape=jax.ShapeDtypeStruct(before.shape, F32),
        name="compose",
    )(before, now)


def shards(tokens, w_proj, w_small, beta_bias, decay_rate, w_out):
    tok_rows = tokens.shape[0]
    heads_here = beta_bias.shape[0]
    mirrors = beta_bias.shape[1]
    each = w_proj.shape[1] // heads_here
    small = jnp.pad(w_small, ((0, 0), (0, LANES - w_small.shape[1])))
    joined = jnp.concatenate([w_proj, small], axis=1)
    weights = lax.all_gather(joined, "ctx", axis=0, tiled=True)
    projected = jnp.dot(tokens, weights, preferred_element_type=F32)
    gates = projected[:, heads_here * each :]
    bias = jnp.pad(beta_bias, ((0, 0), (0, 1))).reshape(1, -1)
    rate = jnp.pad(decay_rate[:, None], ((0, 0), (mirrors, 0))).reshape(1, -1)
    rows = jnp.concatenate([bias, rate], axis=0)
    rows = jnp.pad(rows, ((0, 6), (0, LANES - rows.shape[1])))
    found = [
        local_pass(projected[:, head * each : (head + 1) * each], gates, rows, head)
        for head in range(heads_here)
    ]
    window = jnp.stack([f[0] for f in found])
    queries = jnp.stack([f[1] for f in found])
    partial = jnp.stack([f[2] for f in found])
    by = 1
    count = lax.axis_size("ctx")
    while 2 * by < count:
        window = compose(shift(window, by), window)
        by *= 2
    near = shift(window, 1)
    far = shift(window[:, LANES:], by + 1)
    state_in = compose(far, near)
    normed = pl.pallas_call(
        finish_kernel,
        out_shape=jax.ShapeDtypeStruct((tok_rows, heads_here * LANES), BF16),
        name="finish",
    )(state_in, queries, partial)
    group_count = lax.axis_size("head")
    rows_each = tok_rows // group_count
    stacked = normed.reshape(group_count, rows_each, heads_here * LANES)
    taken = lax.all_to_all(stacked, "head", split_axis=0, concat_axis=0, tiled=True)
    flipped = lax.all_gather(w_out.T, ("head", "ctx"), axis=0, tiled=True)
    flipped = flipped.reshape(group_count, w_out.shape[1] * count, w_out.shape[0])
    mixed = jnp.einsum("hrk,hdk->rd", taken, flipped, preferred_element_type=F32)
    return mixed.astype(BF16)


def solution(mesh):
    placed = (
        P("ctx", None),
        P("ctx", "head"),
        P("ctx", "head"),
        P("head", None),
        P("head"),
        P("head", "ctx"),
    )
    return jax.shard_map(
        shards, mesh=mesh, in_specs=placed, out_specs=P(("ctx", "head"), None), check_vma=False
    )
```

```python
import jax
import jax.numpy as jnp
from jax import lax
from jax.experimental import pallas as pl
from jax.experimental.pallas import tpu as pltpu
from jax.sharding import Mesh
from jax.sharding import PartitionSpec as P

F32 = jnp.float32
BF16 = jnp.bfloat16
LANES = 128
BLOCK = 64
ROWS = (((1,), (0,)), ((), ()))
NT = (((1,), (1,)), ((), ()))
TN = (((0,), (0,)), ((), ()))


def split(array):
    high = array.astype(BF16)
    return high, (array - high.astype(F32)).astype(BF16)


def dot1(left, right, dims):
    return lax.dot_general(left, right, dims, preferred_element_type=F32)


def dot3(left, right, dims):
    return (
        dot1(left[0], right[0], dims)
        + dot1(left[0], right[1], dims)
        + dot1(left[1], right[0], dims)
    )


Y_SIZE = 4
CTX = ("z", "m", "p")


def permute(array, move):
    count = lax.axis_size(CTX)
    z_size = count // Y_SIZE
    pairs = []
    for z in range(z_size):
        for y in range(Y_SIZE):
            to_z, to_y = move(z, y)
            pairs.append((z * Y_SIZE + y, (to_z % z_size) * Y_SIZE + to_y))
    return lax.ppermute(array, CTX, pairs)


def permute_heads(array, move):
    count = lax.axis_size("head")
    return lax.ppermute(array, "head", [(i, move(i) % count) for i in range(count)])


def shift(array, by):
    nodes = lax.axis_size(CTX) // 2

    def place(node, half):
        return node // 2 * Y_SIZE + ((0, 3), (1, 2))[half][node % 2]

    pairs = [(place(n, s), place(n + by, s)) for s in range(2) for n in range(nodes - by)]
    return lax.ppermute(array, CTX, pairs)


def unit(rows):
    return rows / jnp.sqrt(jnp.sum(rows * rows, axis=-1, keepdims=True) + 1e-06)


def local_kernel(swap_ref, proj_ref, row_ref, state_ref, query_ref, out_ref, held_ref):
    del swap_ref
    tokens = proj_ref.shape[0]
    width = LANES
    blocks = tokens // BLOCK
    span = 2 * BLOCK
    gates = proj_ref[:, 5 * width :]
    bias = row_ref[0:1, :]
    rate = row_ref[1:2, :]
    betas = 2.0 / (1.0 + jnp.exp(-(gates + bias)))
    soft = jnp.maximum(gates, 0.0) + jnp.log1p(jnp.exp(-jnp.abs(gates)))
    log_decay = -rate * soft
    row64 = lax.broadcasted_iota(jnp.int32, (BLOCK, BLOCK), 0)
    col64 = lax.broadcasted_iota(jnp.int32, (BLOCK, BLOCK), 1)
    lower = jnp.where(row64 >= col64, 1.0, 0.0).astype(F32)
    base = 0
    row_i = lax.broadcasted_iota(jnp.int32, (span, span), 0)
    col_i = lax.broadcasted_iota(jnp.int32, (span, span), 1)
    row_t, row_r = row_i % BLOCK, row_i // BLOCK
    col_t, col_r = col_i % BLOCK, col_i // BLOCK
    strict = (row_t > col_t) | ((row_t == col_t) & (row_r > col_r))
    within = (row_t == col_t) & (row_r > col_r)
    eye = jnp.where(row_i == col_i, 1.0, 0.0).astype(F32)
    visible = (
        lax.broadcasted_iota(jnp.int32, (BLOCK, span), 0)
        >= lax.broadcasted_iota(jnp.int32, (BLOCK, span), 1) % BLOCK
    )
    levels = []
    size = 1
    while size < BLOCK:
        levels.append(
            (row_t // (2 * size) == col_t // (2 * size))
            & ((row_t // size) % 2 == 1)
            & ((col_t // size) % 2 == 0)
        )
        size *= 2

    def prepare(n):
        rows = slice(n * BLOCK, (n + 1) * BLOCK)
        query = unit(proj_ref[rows, 0:width])
        keys = jnp.concatenate(
            [
                unit(proj_ref[rows, width : 2 * width]),
                unit(proj_ref[rows, 2 * width : 3 * width]),
            ],
            axis=0,
        )
        values = jnp.concatenate(
            [proj_ref[rows, 3 * width : 4 * width], proj_ref[rows, 4 * width : 5 * width]], axis=0
        )
        beta = jnp.concatenate(
            [betas[rows, base : base + 1], betas[rows, base + 1 : base + 2]], axis=0
        )
        running = jnp.dot(
            lower, log_decay[rows], precision=lax.Precision.HIGHEST, preferred_element_type=F32
        )
        across = jnp.transpose(running)[base + 2 : base + 3, :]
        down = running[:, base + 2 : base + 3]
        across = jnp.concatenate([across, across], axis=1)
        reach = jnp.exp(jnp.where(visible, down - across, 0.0))
        keys_s = split(keys)
        both = jnp.concatenate([query, keys], axis=0)
        scores = dot3(split(both), keys_s, NT)
        attend = jnp.where(visible, reach, 0.0) * scores[:BLOCK]
        system = jnp.where(
            strict, beta * jnp.concatenate([reach, reach], axis=0) * scores[BLOCK:], 0.0
        )
        grow = jnp.exp(down)
        grow2 = jnp.concatenate([grow, grow], axis=0)
        last = running[BLOCK - 1 : BLOCK, base + 2 : base + 3]
        tail = jnp.exp(last - down)
        tail2 = jnp.concatenate([tail, tail], axis=0)
        right = jnp.concatenate([beta * grow2 * keys, beta * values], axis=1)
        return dict(
            query=query * grow,
            keys=keys_s,
            attend=attend,
            system=system,
            right=right,
            tail=tail2,
            last=jnp.exp(last),
            inverse=eye - jnp.where(within, system, 0.0),
        )

    parts = [prepare(n) for n in range(blocks)]
    for level in levels:
        for part in parts:
            inverse = split(part["inverse"])
            corner = split(jnp.where(level, part["system"], 0.0))
            middle = dot3(corner, inverse, ROWS)
            part["inverse"] = part["inverse"] - dot3(inverse, split(middle), ROWS)
    for part in parts:
        solved = dot3(split(part["inverse"]), split(part["right"]), ROWS)
        part["step"] = dot3(split(solved * part["tail"]), part["keys"], TN)
        seen = dot3(split(part["attend"]), split(solved), ROWS)
        part["query"] = part["query"] - seen[:, :width]
        part["seen"] = seen[:, width:]
    zero = jnp.zeros((width, width), F32)

    @pl.when(pl.program_id(0) == 0)
    def _():
        held_ref[:width, :] = eye
        held_ref[width:, :] = zero

    state = held_ref[...]
    for n, part in enumerate(parts):
        rows = slice(n * BLOCK, (n + 1) * BLOCK)
        state_s = split(state)
        reads = dot3(split(part["query"]), state_s, NT)
        query_ref[rows, :] = reads[:, :width]
        out_ref[rows, :] = reads[:, width:] + part["seen"]
        move = part["last"] * eye - part["step"][:width]
        state = dot3(state_s, split(move), ROWS)
        state = state + jnp.concatenate([zero, part["step"][width:]], axis=0)
    held_ref[...] = state
    state_ref[...] = state


def local_pass(swap, proj, rows):
    tokens = proj.shape[0] // 2
    half = jax.ShapeDtypeStruct((proj.shape[0], LANES), F32)
    in_order = pl.BlockSpec((tokens, LANES), lambda i, swap: (i, 0))
    return pl.pallas_call(
        local_kernel,
        grid_spec=pltpu.PrefetchScalarGridSpec(
            num_scalar_prefetch=1,
            grid=(2,),
            in_specs=[
                pl.BlockSpec((tokens, proj.shape[1]), lambda i, swap: (i ^ swap[0], 0)),
                pl.BlockSpec(rows.shape, lambda i, swap: (0, 0)),
            ],
            out_specs=[
                pl.BlockSpec((2 * LANES, LANES), lambda i, swap: (0, 0)),
                in_order,
                in_order,
            ],
            scratch_shapes=[pltpu.VMEM((2 * LANES, LANES), F32)],
        ),
        out_shape=(jax.ShapeDtypeStruct((2 * LANES, LANES), F32), half, half),
        name="local",
    )(swap, proj, rows)


def finish_kernel(state_ref, query_ref, part_ref, out_ref):
    total = part_ref[...] + dot3(split(query_ref[...]), split(state_ref[...]), NT)
    scale = jnp.sqrt(jnp.mean(total * total, axis=-1, keepdims=True) + 1e-06)
    out_ref[...] = (total / scale).astype(BF16)


def compose_kernel(before_ref, now_ref, out_ref):
    rows = before_ref.shape[0]
    now = now_ref[...]
    moved = dot3(split(before_ref[...]), split(now[:LANES]), ROWS)
    if rows > LANES:
        out_ref[: rows - LANES] = moved[: rows - LANES]
    out_ref[rows - LANES :] = moved[rows - LANES :] + now[LANES:]


def compose(before, now):
    return pl.pallas_call(
        compose_kernel,
        out_shape=jax.ShapeDtypeStruct(before.shape, F32),
        name="compose",
    )(before, now)


def at(buffer, block, index):
    return lax.dynamic_update_slice_in_dim(buffer, block[None], index, axis=0)


def shards(tokens, w_proj, w_small, beta_bias, decay_rate, w_out):
    tok_rows, depth = tokens.shape
    ctx = lax.axis_index(CTX)
    count = lax.axis_size(CTX)
    z_size = count // Y_SIZE
    z, y = ctx // Y_SIZE, ctx % Y_SIZE
    pair, place = y // 2, y % 2
    second = (y + 1) // 2 % 2 == 1
    group = lax.axis_index("head")
    groups = lax.axis_size("head")
    rows_each = tok_rows // groups
    column, core = group // 2, group % 2
    columns = groups // 2

    flipped = lax.all_gather(w_out.T, ("head",) + CTX, axis=0, tiled=True)
    flipped = flipped.reshape(groups, w_out.shape[1] * count, w_out.shape[0])

    each = w_proj.shape[1] // 2
    gates = w_small.shape[1] // 2
    small = jnp.zeros((w_small.shape[0], LANES - gates), BF16)
    first_half = jnp.concatenate([w_proj[:, :each], w_small[:, :gates], small], axis=1)
    second_half = jnp.concatenate([w_proj[:, each:], w_small[:, gates:], small], axis=1)
    own = jnp.where(second, second_half, first_half)
    other = jnp.where(second, first_half, second_half)

    across = permute(other, lambda z, y: (z, y ^ 1))
    part = lax.dynamic_slice_in_dim(tokens, group * rows_each, rows_each, axis=0)
    part = permute(part, lambda z, y: (z, y ^ 1))
    duo = jnp.where(
        place == 0,
        jnp.concatenate([own, across], axis=0),
        jnp.concatenate([across, own], axis=0),
    )
    mate = permute(duo, lambda z, y: (z, 3 - y))
    quad = jnp.where(
        pair == 0,
        jnp.concatenate([duo, mate], axis=0),
        jnp.concatenate([mate, duo], axis=0),
    )
    weights = jnp.zeros((z_size,) + quad.shape, BF16)
    weights = at(weights, quad, z)
    parts = jnp.zeros((columns,) + part.shape, BF16)
    parts = at(parts, part, column)
    up = down = quad
    for step in range(1, z_size // 2):
        up = permute(up, lambda z, y: (z + 1, y))
        down = permute(down, lambda z, y: (z - 1, y))
        weights = at(weights, up, (z - step) % z_size)
        weights = at(weights, down, (z + step) % z_size)
    up = permute(up, lambda z, y: (z + 1, y))
    weights = at(weights, up, (z - z_size // 2) % z_size)
    for step in range(1, columns):
        moved = permute_heads(part, lambda i, step=step: i + 2 * step)
        parts = at(parts, moved, (column - step) % columns)
    theirs = permute_heads(parts, lambda i: i ^ 1)
    even = jnp.where(core == 0, parts, theirs)
    odd = jnp.where(core == 0, theirs, parts)
    partner = jnp.stack([even, odd], axis=1).reshape(tok_rows, depth)
    both = jnp.concatenate([tokens, partner], axis=0)
    weights = weights.reshape(depth, quad.shape[1])
    projected = jnp.dot(both, weights, preferred_element_type=F32)

    bias = jnp.where(second, beta_bias[1], beta_bias[0])
    rate = jnp.where(second, decay_rate[1:], decay_rate[:1])
    rows = jnp.stack(
        [
            jnp.pad(bias, (0, LANES - bias.shape[0])),
            jnp.pad(rate, (bias.shape[0], LANES - bias.shape[0] - 1)),
        ]
    )
    rows = jnp.pad(rows, ((0, 6), (0, 0)))
    window, queries, partial = local_pass(place.reshape(1), projected, rows)
    by = 1
    while 4 * by < count:
        window = compose(shift(window, by), window)
        by *= 2
    near = shift(window, 1)
    far = shift(window[LANES:], by + 1)
    state_in = compose(far, near)
    normed = pl.pallas_call(
        finish_kernel,
        out_shape=jax.ShapeDtypeStruct((2 * tok_rows, LANES), BF16),
        name="finish",
    )(state_in, queries, partial)
    stacked = normed.reshape(2 * groups, rows_each, LANES)
    taken = lax.all_to_all(stacked, ("p", "head"), split_axis=0, concat_axis=0, tiled=True)
    taken = taken.reshape(2, groups, rows_each, LANES)
    taken = jnp.where(pair == 0, taken, taken[::-1])
    taken = jnp.concatenate([taken[0], taken[1]], axis=2)
    mixed = jnp.einsum("hrk,hdk->rd", taken, flipped, preferred_element_type=F32)
    return mixed.astype(BF16)


def solution(mesh):
    sizes = dict(mesh.shape)
    finer = Mesh(
        mesh.devices.reshape(sizes["ctx"] // Y_SIZE, 2, 2, sizes["head"]), CTX + ("head",)
    )
    placed = (
        P(CTX, None),
        P(CTX, "head"),
        P(CTX, "head"),
        P("head", None),
        P("head"),
        P("head", CTX),
    )
    return jax.shard_map(
        shards, mesh=finer, in_specs=placed, out_specs=P(CTX + ("head",), None), check_vma=False
    )
```

```python
import jax
import jax.numpy as jnp
from jax import lax
from jax.experimental import pallas as pl
from jax.experimental.pallas import tpu as pltpu
from jax.sharding import Mesh
from jax.sharding import PartitionSpec as P

F32 = jnp.float32
BF16 = jnp.bfloat16
LANES = 128
BLOCK = 64
ROWS = (((1,), (0,)), ((), ()))
NT = (((1,), (1,)), ((), ()))
TN = (((0,), (0,)), ((), ()))


def split(array):
    high = array.astype(BF16)
    return high, (array - high.astype(F32)).astype(BF16)


def dot1(left, right, dims):
    return lax.dot_general(left, right, dims, preferred_element_type=F32)


def dot3(left, right, dims):
    (lc,), (rc,) = dims[0]
    kept = right[0].shape[1 - rc]
    lhs = jnp.concatenate(left, axis=lc)
    if kept == LANES:
        rhs = jnp.concatenate(right, axis=1 - rc)
        rhs = jnp.concatenate([rhs, rhs], axis=rc)
        out = dot1(lhs, rhs, dims)
        return out[:, :LANES] + out[:, LANES:]
    rhs = jnp.concatenate([right[0], right[0]], axis=rc)
    return dot1(lhs, rhs, dims) + dot1(left[0], right[1], dims)


Y_SIZE = 4
CTX = ("z", "m", "p")


def permute(array, move):
    count = lax.axis_size(CTX)
    z_size = count // Y_SIZE
    pairs = []
    for z in range(z_size):
        for y in range(Y_SIZE):
            to_z, to_y = move(z, y)
            pairs.append((z * Y_SIZE + y, (to_z % z_size) * Y_SIZE + to_y))
    return lax.ppermute(array, CTX, pairs)


def permute_heads(array, move):
    count = lax.axis_size("head")
    return lax.ppermute(array, "head", [(i, move(i) % count) for i in range(count)])


def shift(array, by):
    nodes = lax.axis_size(CTX) // 2

    def place(node, half):
        return node // 2 * Y_SIZE + ((0, 3), (1, 2))[half][node % 2]

    pairs = [(place(n, s), place(n + by, s)) for s in range(2) for n in range(nodes - by)]
    return lax.ppermute(array, CTX, pairs)


def unit(rows):
    return rows / jnp.sqrt(jnp.sum(rows * rows, axis=-1, keepdims=True) + 1e-06)


def local_kernel(swap_ref, proj_ref, row_ref, state_ref, query_ref, out_ref, held_ref):
    del swap_ref
    tokens = proj_ref.shape[0]
    width = LANES
    blocks = tokens // BLOCK
    span = 2 * BLOCK
    gates = proj_ref[:, 5 * width :]
    bias = row_ref[0:1, :]
    rate = row_ref[1:2, :]
    betas = 2.0 / (1.0 + jnp.exp(-(gates + bias)))
    soft = jnp.maximum(gates, 0.0) + jnp.log1p(jnp.exp(-jnp.abs(gates)))
    log_decay = -rate * soft
    row64 = lax.broadcasted_iota(jnp.int32, (BLOCK, BLOCK), 0)
    col64 = lax.broadcasted_iota(jnp.int32, (BLOCK, BLOCK), 1)
    lower = jnp.where(row64 >= col64, 1.0, 0.0).astype(F32)
    base = 0
    row_i = lax.broadcasted_iota(jnp.int32, (span, span), 0)
    col_i = lax.broadcasted_iota(jnp.int32, (span, span), 1)
    row_t, row_r = row_i % BLOCK, row_i // BLOCK
    col_t, col_r = col_i % BLOCK, col_i // BLOCK
    strict = (row_t > col_t) | ((row_t == col_t) & (row_r > col_r))
    within = (row_t == col_t) & (row_r > col_r)
    eye = jnp.where(row_i == col_i, 1.0, 0.0).astype(F32)
    visible = (
        lax.broadcasted_iota(jnp.int32, (BLOCK, span), 0)
        >= lax.broadcasted_iota(jnp.int32, (BLOCK, span), 1) % BLOCK
    )
    levels = []
    size = 1
    while size < BLOCK:
        levels.append(
            (row_t // (2 * size) == col_t // (2 * size))
            & ((row_t // size) % 2 == 1)
            & ((col_t // size) % 2 == 0)
        )
        size *= 2

    def prepare(n):
        rows = slice(n * BLOCK, (n + 1) * BLOCK)
        query = unit(proj_ref[rows, 0:width])
        keys = jnp.concatenate(
            [
                unit(proj_ref[rows, width : 2 * width]),
                unit(proj_ref[rows, 2 * width : 3 * width]),
            ],
            axis=0,
        )
        values = jnp.concatenate(
            [proj_ref[rows, 3 * width : 4 * width], proj_ref[rows, 4 * width : 5 * width]], axis=0
        )
        beta = jnp.concatenate(
            [betas[rows, base : base + 1], betas[rows, base + 1 : base + 2]], axis=0
        )
        running = jnp.dot(
            lower, log_decay[rows], precision=lax.Precision.HIGHEST, preferred_element_type=F32
        )
        across = jnp.transpose(running)[base + 2 : base + 3, :]
        down = running[:, base + 2 : base + 3]
        across = jnp.concatenate([across, across], axis=1)
        reach = jnp.exp(jnp.where(visible, down - across, 0.0))
        keys_s = split(keys)
        both = jnp.concatenate([query, keys], axis=0)
        scores = dot3(split(both), keys_s, NT)
        attend = jnp.where(visible, reach, 0.0) * scores[:BLOCK]
        system = jnp.where(
            strict, beta * jnp.concatenate([reach, reach], axis=0) * scores[BLOCK:], 0.0
        )
        grow = jnp.exp(down)
        grow2 = jnp.concatenate([grow, grow], axis=0)
        last = running[BLOCK - 1 : BLOCK, base + 2 : base + 3]
        tail = jnp.exp(last - down)
        tail2 = jnp.concatenate([tail, tail], axis=0)
        right = jnp.concatenate([beta * grow2 * keys, beta * values], axis=1)
        return dict(
            query=query * grow,
            keys=keys_s,
            attend=attend,
            system=system,
            right=right,
            tail=tail2,
            last=jnp.exp(last),
            inverse=eye - jnp.where(within, system, 0.0),
        )

    parts = [prepare(n) for n in range(blocks)]
    for level in levels:
        for part in parts:
            inverse = split(part["inverse"])
            corner = split(jnp.where(level, part["system"], 0.0))
            middle = dot3(corner, inverse, ROWS)
            part["inverse"] = part["inverse"] - dot3(inverse, split(middle), ROWS)
    for part in parts:
        solved = dot3(split(part["inverse"]), split(part["right"]), ROWS)
        part["step"] = dot3(split(solved * part["tail"]), part["keys"], TN)
        seen = dot3(split(part["attend"]), split(solved), ROWS)
        part["query"] = part["query"] - seen[:, :width]
        part["seen"] = seen[:, width:]
    zero = jnp.zeros((width, width), F32)

    @pl.when(pl.program_id(0) == 0)
    def _():
        held_ref[:width, :] = eye
        held_ref[width:, :] = zero

    state = held_ref[...]
    for n, part in enumerate(parts):
        rows = slice(n * BLOCK, (n + 1) * BLOCK)
        state_s = split(state)
        reads = dot3(split(part["query"]), state_s, NT)
        query_ref[rows, :] = reads[:, :width]
        out_ref[rows, :] = reads[:, width:] + part["seen"]
        move = part["last"] * eye - part["step"][:width]
        state = dot3(state_s, split(move), ROWS)
        state = state + jnp.concatenate([zero, part["step"][width:]], axis=0)
    held_ref[...] = state
    state_ref[...] = state


def local_pass(swap, proj, rows):
    tokens = proj.shape[0] // 2
    half = jax.ShapeDtypeStruct((proj.shape[0], LANES), F32)
    in_order = pl.BlockSpec((tokens, LANES), lambda i, swap: (i, 0))
    return pl.pallas_call(
        local_kernel,
        grid_spec=pltpu.PrefetchScalarGridSpec(
            num_scalar_prefetch=1,
            grid=(2,),
            in_specs=[
                pl.BlockSpec((tokens, proj.shape[1]), lambda i, swap: (i ^ swap[0], 0)),
                pl.BlockSpec(rows.shape, lambda i, swap: (0, 0)),
            ],
            out_specs=[
                pl.BlockSpec((2 * LANES, LANES), lambda i, swap: (0, 0)),
                in_order,
                in_order,
            ],
            scratch_shapes=[pltpu.VMEM((2 * LANES, LANES), F32)],
        ),
        out_shape=(jax.ShapeDtypeStruct((2 * LANES, LANES), F32), half, half),
        name="local",
    )(swap, proj, rows)


def finish_kernel(state_ref, query_ref, part_ref, out_ref):
    total = part_ref[...] + dot3(split(query_ref[...]), split(state_ref[...]), NT)
    scale = jnp.sqrt(jnp.mean(total * total, axis=-1, keepdims=True) + 1e-06)
    out_ref[...] = (total / scale).astype(BF16)


def compose(before, now):
    moved = jnp.matmul(before, now[:LANES], precision=lax.Precision.HIGHEST)
    kept = lax.broadcasted_iota(jnp.int32, now.shape, 0) >= LANES
    return moved + jnp.where(kept, now, 0.0)[-before.shape[0] :]


def at(buffer, block, index):
    return lax.dynamic_update_slice_in_dim(buffer, block[None], index, axis=0)


def shards(tokens, w_proj, w_small, beta_bias, decay_rate, w_out):
    tok_rows, depth = tokens.shape
    ctx = lax.axis_index(CTX)
    count = lax.axis_size(CTX)
    z_size = count // Y_SIZE
    z, y = ctx // Y_SIZE, ctx % Y_SIZE
    pair, place = y // 2, y % 2
    second = (y + 1) // 2 % 2 == 1
    group = lax.axis_index("head")
    groups = lax.axis_size("head")
    rows_each = tok_rows // groups
    column, core = group // 2, group % 2
    columns = groups // 2

    flipped = lax.all_gather(w_out.T, ("head",) + CTX, axis=0, tiled=True)
    flipped = flipped.reshape(groups, w_out.shape[1] * count, w_out.shape[0])

    each = w_proj.shape[1] // 2
    gates = w_small.shape[1] // 2
    small = jnp.zeros((w_small.shape[0], LANES - gates), BF16)
    first_half = jnp.concatenate([w_proj[:, :each], w_small[:, :gates], small], axis=1)
    second_half = jnp.concatenate([w_proj[:, each:], w_small[:, gates:], small], axis=1)
    own = jnp.where(second, second_half, first_half)
    other = jnp.where(second, first_half, second_half)

    part = lax.dynamic_slice_in_dim(tokens, group * rows_each, rows_each, axis=0)
    part = permute(part, lambda z, y: (z, y ^ 1))
    quad = jnp.zeros((Y_SIZE,) + own.shape, BF16)
    quad = at(quad, own, y)
    for flip, block in ((3, own), (1, other), (2, other)):
        came = permute(block, lambda z, y, flip=flip: (z, y ^ flip))
        quad = at(quad, came, y ^ flip)
    quad = quad.reshape(Y_SIZE * own.shape[0], own.shape[1])
    weights = jnp.zeros((z_size,) + quad.shape, BF16)
    weights = at(weights, quad, z)
    parts = jnp.zeros((columns,) + part.shape, BF16)
    parts = at(parts, part, column)
    up = down = quad
    for step in range(1, z_size // 2):
        up = permute(up, lambda z, y: (z + 1, y))
        down = permute(down, lambda z, y: (z - 1, y))
        weights = at(weights, up, (z - step) % z_size)
        weights = at(weights, down, (z + step) % z_size)
    middle = quad.shape[0] // 2
    last = jnp.concatenate(
        [
            permute(up[:middle], lambda z, y: (z + 1, y)),
            permute(down[middle:], lambda z, y: (z - 1, y)),
        ],
        axis=0,
    )
    weights = at(weights, last, (z + z_size // 2) % z_size)
    for step in range(1, columns):
        moved = permute_heads(part, lambda i, step=step: i + 2 * step)
        parts = at(parts, moved, (column - step) % columns)
    theirs = permute_heads(parts, lambda i: i ^ 1)
    even = jnp.where(core == 0, parts, theirs)
    odd = jnp.where(core == 0, theirs, parts)
    partner = jnp.stack([even, odd], axis=1).reshape(tok_rows, depth)
    both = jnp.concatenate([tokens, partner], axis=0)
    weights = weights.reshape(depth, quad.shape[1])
    projected = jnp.dot(both, weights, preferred_element_type=F32)

    bias = jnp.where(second, beta_bias[1], beta_bias[0])
    rate = jnp.where(second, decay_rate[1:], decay_rate[:1])
    rows = jnp.stack(
        [
            jnp.pad(bias, (0, LANES - bias.shape[0])),
            jnp.pad(rate, (bias.shape[0], LANES - bias.shape[0] - 1)),
        ]
    )
    rows = jnp.pad(rows, ((0, 6), (0, 0)))
    window, queries, partial = local_pass(place.reshape(1), projected, rows)
    by = 1
    while 4 * by < count:
        window = compose(shift(window, by), window)
        by *= 2
    near = shift(window, 1)
    far = shift(window[LANES:], by + 1)
    state_in = compose(far, near)
    normed = pl.pallas_call(
        finish_kernel,
        out_shape=jax.ShapeDtypeStruct((2 * tok_rows, LANES), BF16),
        name="finish",
    )(state_in, queries, partial)
    stacked = normed.reshape(2 * groups, rows_each, LANES)
    taken = lax.all_to_all(stacked, ("p", "head"), split_axis=0, concat_axis=0, tiled=True)
    taken = taken.reshape(2, groups, rows_each, LANES)
    taken = jnp.where(pair == 0, taken, taken[::-1])
    taken = jnp.concatenate([taken[0], taken[1]], axis=2)
    mixed = jnp.einsum("hrk,hdk->rd", taken, flipped, preferred_element_type=F32)
    return mixed.astype(BF16)


def solution(mesh):
    sizes = dict(mesh.shape)
    finer = Mesh(
        mesh.devices.reshape(sizes["ctx"] // Y_SIZE, 2, 2, sizes["head"]), CTX + ("head",)
    )
    placed = (
        P(CTX, None),
        P(CTX, "head"),
        P(CTX, "head"),
        P("head", None),
        P("head"),
        P("head", CTX),
    )
    return jax.shard_map(
        shards, mesh=finer, in_specs=placed, out_specs=P(CTX + ("head",), None), check_vma=False
    )
```

```python
import jax
import jax.numpy as jnp
from jax import lax
from jax.experimental import pallas as pl
from jax.experimental.pallas import tpu as pltpu
from jax.sharding import Mesh
from jax.sharding import PartitionSpec as P

F32 = jnp.float32
BF16 = jnp.bfloat16
LANES = 128
BLOCK = 64
ROWS = (((1,), (0,)), ((), ()))
NT = (((1,), (1,)), ((), ()))
TN = (((0,), (0,)), ((), ()))


def split(array):
    high = array.astype(BF16)
    return high, (array - high.astype(F32)).astype(BF16)


def dot1(left, right, dims):
    return lax.dot_general(left, right, dims, preferred_element_type=F32)


def dot3(left, right, dims):
    (lc,), (rc,) = dims[0]
    kept = right[0].shape[1 - rc]
    lhs = jnp.concatenate(left, axis=lc)
    if kept == LANES:
        rhs = jnp.concatenate(right, axis=1 - rc)
        rhs = jnp.concatenate([rhs, rhs], axis=rc)
        out = dot1(lhs, rhs, dims)
        return out[:, :LANES] + out[:, LANES:]
    rhs = jnp.concatenate([right[0], right[0]], axis=rc)
    return dot1(lhs, rhs, dims) + dot1(left[0], right[1], dims)


Y_SIZE = 4
CTX = ("z", "m", "p")


def permute(array, move):
    count = lax.axis_size(CTX)
    z_size = count // Y_SIZE
    pairs = []
    for z in range(z_size):
        for y in range(Y_SIZE):
            to_z, to_y = move(z, y)
            pairs.append((z * Y_SIZE + y, (to_z % z_size) * Y_SIZE + to_y))
    return lax.ppermute(array, CTX, pairs)


def permute_heads(array, move):
    count = lax.axis_size("head")
    return lax.ppermute(array, "head", [(i, move(i) % count) for i in range(count)])


def shift(array, by):
    nodes = lax.axis_size(CTX) // 2

    def place(node, half):
        return node // 2 * Y_SIZE + ((0, 3), (1, 2))[half][node % 2]

    pairs = [(place(n, s), place(n + by, s)) for s in range(2) for n in range(nodes - by)]
    return lax.ppermute(array, CTX, pairs)


def unit(rows):
    return rows / jnp.sqrt(jnp.sum(rows * rows, axis=-1, keepdims=True) + 1e-06)


def running_decay(gates, row_ref):
    soft = jnp.maximum(gates, 0.0) + jnp.log1p(jnp.exp(-jnp.abs(gates)))
    log_decay = -row_ref[1:2, :] * soft
    row = lax.broadcasted_iota(jnp.int32, (BLOCK, BLOCK), 0)
    col = lax.broadcasted_iota(jnp.int32, (BLOCK, BLOCK), 1)
    lower = jnp.where(row >= col, 1.0, 0.0).astype(F32)
    return [
        jnp.dot(
            lower,
            log_decay[n * BLOCK : (n + 1) * BLOCK],
            precision=lax.Precision.HIGHEST,
            preferred_element_type=F32,
        )
        for n in range(gates.shape[0] // BLOCK)
    ]


def seen_before():
    return (
        lax.broadcasted_iota(jnp.int32, (BLOCK, 2 * BLOCK), 0)
        >= lax.broadcasted_iota(jnp.int32, (BLOCK, 2 * BLOCK), 1) % BLOCK
    )


def reach_of(running, visible):
    across = jnp.transpose(running)[2:3, :]
    across = jnp.concatenate([across, across], axis=1)
    return jnp.exp(jnp.where(visible, running[:, 2:3] - across, 0.0))


def keys_of(proj_ref, rows):
    return jnp.concatenate(
        [
            unit(proj_ref[rows, LANES : 2 * LANES]),
            unit(proj_ref[rows, 2 * LANES : 3 * LANES]),
        ],
        axis=0,
    )


def local_kernel(swap_ref, proj_ref, row_ref, state_ref, solved_ref, starts_ref, held_ref):
    del swap_ref
    tokens = proj_ref.shape[0]
    width = LANES
    blocks = tokens // BLOCK
    span = 2 * BLOCK
    gates = proj_ref[:, 5 * width :]
    betas = 2.0 / (1.0 + jnp.exp(-(gates + row_ref[0:1, :])))
    runnings = running_decay(gates, row_ref)
    row_i = lax.broadcasted_iota(jnp.int32, (span, span), 0)
    col_i = lax.broadcasted_iota(jnp.int32, (span, span), 1)
    row_t, row_r = row_i % BLOCK, row_i // BLOCK
    col_t, col_r = col_i % BLOCK, col_i // BLOCK
    strict = (row_t > col_t) | ((row_t == col_t) & (row_r > col_r))
    within = (row_t == col_t) & (row_r > col_r)
    eye = jnp.where(row_i == col_i, 1.0, 0.0).astype(F32)
    visible = seen_before()
    levels = []
    size = 1
    while size < BLOCK:
        levels.append(
            (row_t // (2 * size) == col_t // (2 * size))
            & ((row_t // size) % 2 == 1)
            & ((col_t // size) % 2 == 0)
        )
        size *= 2

    def prepare(n):
        rows = slice(n * BLOCK, (n + 1) * BLOCK)
        keys = keys_of(proj_ref, rows)
        values = jnp.concatenate(
            [proj_ref[rows, 3 * width : 4 * width], proj_ref[rows, 4 * width : 5 * width]], axis=0
        )
        beta = jnp.concatenate([betas[rows, 0:1], betas[rows, 1:2]], axis=0)
        running = runnings[n]
        reach = reach_of(running, visible)
        keys_s = split(keys)
        scores = dot3(keys_s, keys_s, NT)
        system = jnp.where(strict, beta * jnp.concatenate([reach, reach], axis=0) * scores, 0.0)
        down = running[:, 2:3]
        grow = jnp.exp(down)
        grow2 = jnp.concatenate([grow, grow], axis=0)
        last = running[BLOCK - 1 : BLOCK, 2:3]
        tail = jnp.exp(last - down)
        return dict(
            keys=keys_s,
            system=system,
            right=jnp.concatenate([beta * grow2 * keys, beta * values], axis=1),
            tail=jnp.concatenate([tail, tail], axis=0),
            last=jnp.exp(last),
            inverse=eye - jnp.where(within, system, 0.0),
        )

    parts = [prepare(n) for n in range(blocks)]
    for level in levels:
        for part in parts:
            inverse = split(part["inverse"])
            corner = split(jnp.where(level, part["system"], 0.0))
            middle = dot3(corner, inverse, ROWS)
            part["inverse"] = part["inverse"] - dot3(inverse, split(middle), ROWS)
    for n, part in enumerate(parts):
        solved = dot3(split(part["inverse"]), split(part["right"]), ROWS)
        solved_ref[n] = solved
        part["step"] = dot3(split(solved * part["tail"]), part["keys"], TN)
    zero = jnp.zeros((width, width), F32)

    @pl.when(pl.program_id(0) == 0)
    def _():
        held_ref[:width, :] = eye
        held_ref[width:, :] = zero

    state = held_ref[...]
    for n, part in enumerate(parts):
        starts_ref[n] = state
        move = part["last"] * eye - part["step"][:width]
        state = dot3(split(state), split(move), ROWS)
        state = state + jnp.concatenate([zero, part["step"][width:]], axis=0)
    held_ref[...] = state
    state_ref[...] = state


def read_kernel(swap_ref, proj_ref, row_ref, solved_ref, starts_ref, query_ref, out_ref):
    del swap_ref
    width = LANES
    visible = seen_before()
    runnings = running_decay(proj_ref[:, 5 * width :], row_ref)
    for n, running in enumerate(runnings):
        rows = slice(n * BLOCK, (n + 1) * BLOCK)
        query = unit(proj_ref[rows, 0:width])
        scores = dot3(split(query), split(keys_of(proj_ref, rows)), NT)
        attend = jnp.where(visible, reach_of(running, visible), 0.0) * scores
        seen = dot3(split(attend), split(solved_ref[n]), ROWS)
        query = query * jnp.exp(running[:, 2:3]) - seen[:, :width]
        reads = dot3(split(query), split(starts_ref[n]), NT)
        query_ref[rows, :] = reads[:, :width]
        out_ref[rows, :] = reads[:, width:] + seen[:, width:]


def local_pass(swap, proj, rows):
    tokens = proj.shape[0] // 2
    blocks = tokens // BLOCK
    saved = jax.ShapeDtypeStruct((2 * blocks, 2 * LANES, LANES), F32)
    wide = jax.ShapeDtypeStruct((2 * blocks, LANES, 2 * LANES), F32)
    half = jax.ShapeDtypeStruct((proj.shape[0], LANES), F32)
    own_order = pl.BlockSpec((tokens, proj.shape[1]), lambda i, swap: (i ^ swap[0], 0))
    table = pl.BlockSpec(rows.shape, lambda i, swap: (0, 0))
    saved_spec = pl.BlockSpec((blocks, 2 * LANES, LANES), lambda i, swap: (i, 0, 0))
    wide_spec = pl.BlockSpec((blocks, LANES, 2 * LANES), lambda i, swap: (i, 0, 0))
    half_spec = pl.BlockSpec((tokens, LANES), lambda i, swap: (i, 0))
    window, solved, starts = pl.pallas_call(
        local_kernel,
        grid_spec=pltpu.PrefetchScalarGridSpec(
            num_scalar_prefetch=1,
            grid=(2,),
            in_specs=[own_order, table],
            out_specs=[
                pl.BlockSpec((2 * LANES, LANES), lambda i, swap: (0, 0)),
                wide_spec,
                saved_spec,
            ],
            scratch_shapes=[pltpu.VMEM((2 * LANES, LANES), F32)],
        ),
        out_shape=(jax.ShapeDtypeStruct((2 * LANES, LANES), F32), wide, saved),
        name="local",
    )(swap, proj, rows)
    queries, partial = pl.pallas_call(
        read_kernel,
        grid_spec=pltpu.PrefetchScalarGridSpec(
            num_scalar_prefetch=1,
            grid=(2,),
            in_specs=[own_order, table, wide_spec, saved_spec],
            out_specs=[half_spec, half_spec],
        ),
        out_shape=(half, half),
        name="reads",
    )(swap, proj, rows, solved, starts)
    return window, queries, partial


def finish_kernel(state_ref, query_ref, part_ref, out_ref):
    total = part_ref[...] + dot3(split(query_ref[...]), split(state_ref[...]), NT)
    scale = jnp.sqrt(jnp.mean(total * total, axis=-1, keepdims=True) + 1e-06)
    out_ref[...] = (total / scale).astype(BF16)


def compose(before, now):
    moved = jnp.matmul(before, now[:LANES], precision=lax.Precision.HIGHEST)
    kept = lax.broadcasted_iota(jnp.int32, now.shape, 0) >= LANES
    return moved + jnp.where(kept, now, 0.0)[-before.shape[0] :]


def at(buffer, block, index):
    return lax.dynamic_update_slice_in_dim(buffer, block[None], index, axis=0)


def shards(tokens, w_proj, w_small, beta_bias, decay_rate, w_out):
    tok_rows, depth = tokens.shape
    ctx = lax.axis_index(CTX)
    count = lax.axis_size(CTX)
    z_size = count // Y_SIZE
    z, y = ctx // Y_SIZE, ctx % Y_SIZE
    pair, place = y // 2, y % 2
    second = (y + 1) // 2 % 2 == 1
    group = lax.axis_index("head")
    groups = lax.axis_size("head")
    rows_each = tok_rows // groups
    column, core = group // 2, group % 2
    columns = groups // 2

    flipped = lax.all_gather(w_out.T, ("head",) + CTX, axis=0, tiled=True)
    flipped = flipped.reshape(groups, w_out.shape[1] * count, w_out.shape[0])

    each = w_proj.shape[1] // 2
    gates = w_small.shape[1] // 2
    small = jnp.zeros((w_small.shape[0], LANES - gates), BF16)
    first_half = jnp.concatenate([w_proj[:, :each], w_small[:, :gates], small], axis=1)
    second_half = jnp.concatenate([w_proj[:, each:], w_small[:, gates:], small], axis=1)
    own = jnp.where(second, second_half, first_half)
    other = jnp.where(second, first_half, second_half)

    part = lax.dynamic_slice_in_dim(tokens, group * rows_each, rows_each, axis=0)
    part = permute(part, lambda z, y: (z, y ^ 1))
    quad = jnp.zeros((Y_SIZE,) + own.shape, BF16)
    quad = at(quad, own, y)
    for flip, block in ((3, own), (1, other), (2, other)):
        came = permute(block, lambda z, y, flip=flip: (z, y ^ flip))
        quad = at(quad, came, y ^ flip)
    quad = quad.reshape(Y_SIZE * own.shape[0], own.shape[1])
    weights = jnp.zeros((z_size,) + quad.shape, BF16)
    weights = at(weights, quad, z)
    parts = jnp.zeros((columns,) + part.shape, BF16)
    parts = at(parts, part, column)
    up = down = quad
    for step in range(1, z_size // 2):
        up = permute(up, lambda z, y: (z + 1, y))
        down = permute(down, lambda z, y: (z - 1, y))
        weights = at(weights, up, (z - step) % z_size)
        weights = at(weights, down, (z + step) % z_size)
    middle = quad.shape[0] // 2
    last = jnp.concatenate(
        [
            permute(up[:middle], lambda z, y: (z + 1, y)),
            permute(down[middle:], lambda z, y: (z - 1, y)),
        ],
        axis=0,
    )
    opposite = (z + z_size // 2) % z_size
    for step in range(1, columns):
        moved = permute_heads(part, lambda i, step=step: i + 2 * step)
        parts = at(parts, moved, (column - step) % columns)
    theirs = permute_heads(parts, lambda i: i ^ 1)
    even = jnp.where(core == 0, parts, theirs)
    odd = jnp.where(core == 0, theirs, parts)
    partner = jnp.stack([even, odd], axis=1).reshape(tok_rows, depth)
    both = jnp.concatenate([tokens, partner], axis=0)
    weights = weights.reshape(depth, quad.shape[1])
    projected = jnp.dot(both, weights, preferred_element_type=F32)
    behind = lax.dynamic_slice_in_dim(both, opposite * quad.shape[0], quad.shape[0], axis=1)
    projected = projected + jnp.dot(behind, last, preferred_element_type=F32)

    bias = jnp.where(second, beta_bias[1], beta_bias[0])
    rate = jnp.where(second, decay_rate[1:], decay_rate[:1])
    rows = jnp.stack(
        [
            jnp.pad(bias, (0, LANES - bias.shape[0])),
            jnp.pad(rate, (bias.shape[0], LANES - bias.shape[0] - 1)),
        ]
    )
    rows = jnp.pad(rows, ((0, 6), (0, 0)))
    window, queries, partial = local_pass(place.reshape(1), projected, rows)
    by = 1
    while 4 * by < count:
        before = shift(window, by)
        if by == 1:
            before, queries, partial = lax.optimization_barrier((before, queries, partial))
        window = compose(before, window)
        by *= 2
    near = shift(window, 1)
    far = shift(window[LANES:], by + 1)
    state_in = compose(far, near)
    normed = pl.pallas_call(
        finish_kernel,
        out_shape=jax.ShapeDtypeStruct((2 * tok_rows, LANES), BF16),
        name="finish",
    )(state_in, queries, partial)
    stacked = normed.reshape(2 * groups, rows_each, LANES)
    taken = lax.all_to_all(stacked, ("p", "head"), split_axis=0, concat_axis=0, tiled=True)
    taken = taken.reshape(2, groups, rows_each, LANES)
    taken = jnp.where(pair == 0, taken, taken[::-1])
    taken = jnp.concatenate([taken[0], taken[1]], axis=2)
    mixed = jnp.einsum("hrk,hdk->rd", taken, flipped, preferred_element_type=F32)
    return mixed.astype(BF16)


def solution(mesh):
    sizes = dict(mesh.shape)
    finer = Mesh(
        mesh.devices.reshape(sizes["ctx"] // Y_SIZE, 2, 2, sizes["head"]), CTX + ("head",)
    )
    placed = (
        P(CTX, None),
        P(CTX, "head"),
        P(CTX, "head"),
        P("head", None),
        P("head"),
        P("head", CTX),
    )
    return jax.shard_map(
        shards, mesh=finer, in_specs=placed, out_specs=P(CTX + ("head",), None), check_vma=False
    )
```

```python
import jax
import jax.numpy as jnp
from jax import lax
from jax.experimental import pallas as pl
from jax.experimental.pallas import tpu as pltpu
from jax.sharding import Mesh
from jax.sharding import PartitionSpec as P

F32 = jnp.float32
BF16 = jnp.bfloat16
LANES = 128
BLOCK = 64
ROWS = (((1,), (0,)), ((), ()))
NT = (((1,), (1,)), ((), ()))
TN = (((0,), (0,)), ((), ()))


def split(array):
    high = array.astype(BF16)
    return high, (array - high.astype(F32)).astype(BF16)


def dot1(left, right, dims):
    return lax.dot_general(left, right, dims, preferred_element_type=F32)


def dot3(left, right, dims):
    (lc,), (rc,) = dims[0]
    kept = right[0].shape[1 - rc]
    lhs = jnp.concatenate(left, axis=lc)
    if kept == LANES:
        rhs = jnp.concatenate(right, axis=1 - rc)
        rhs = jnp.concatenate([rhs, rhs], axis=rc)
        out = dot1(lhs, rhs, dims)
        return out[:, :LANES] + out[:, LANES:]
    rhs = jnp.concatenate([right[0], right[0]], axis=rc)
    return dot1(lhs, rhs, dims) + dot1(left[0], right[1], dims)


Y_SIZE = 4
CTX = ("z", "m", "p")


def permute(array, move):
    count = lax.axis_size(CTX)
    z_size = count // Y_SIZE
    pairs = []
    for z in range(z_size):
        for y in range(Y_SIZE):
            to_z, to_y = move(z, y)
            pairs.append((z * Y_SIZE + y, (to_z % z_size) * Y_SIZE + to_y))
    return lax.ppermute(array, CTX, pairs)


def permute_heads(array, move):
    count = lax.axis_size("head")
    return lax.ppermute(array, "head", [(i, move(i) % count) for i in range(count)])


def shift(array, by):
    nodes = lax.axis_size(CTX) // 2

    def place(node, half):
        return node // 2 * Y_SIZE + ((0, 3), (1, 2))[half][node % 2]

    pairs = [(place(n, s), place(n + by, s)) for s in range(2) for n in range(nodes - by)]
    return lax.ppermute(array, CTX, pairs)


def unit(rows):
    return rows / jnp.sqrt(jnp.sum(rows * rows, axis=-1, keepdims=True) + 1e-06)


def running_decay(gates, row_ref):
    soft = jnp.maximum(gates, 0.0) + jnp.log1p(jnp.exp(-jnp.abs(gates)))
    log_decay = -row_ref[1:2, :] * soft
    row = lax.broadcasted_iota(jnp.int32, (BLOCK, BLOCK), 0)
    col = lax.broadcasted_iota(jnp.int32, (BLOCK, BLOCK), 1)
    lower = jnp.where(row >= col, 1.0, 0.0).astype(F32)
    return [
        jnp.dot(
            lower,
            log_decay[n * BLOCK : (n + 1) * BLOCK],
            precision=lax.Precision.HIGHEST,
            preferred_element_type=F32,
        )
        for n in range(gates.shape[0] // BLOCK)
    ]


def seen_before():
    return (
        lax.broadcasted_iota(jnp.int32, (BLOCK, 2 * BLOCK), 0)
        >= lax.broadcasted_iota(jnp.int32, (BLOCK, 2 * BLOCK), 1) % BLOCK
    )


def reach_of(running, visible):
    across = jnp.transpose(running)[2:3, :]
    across = jnp.concatenate([across, across], axis=1)
    return jnp.exp(jnp.where(visible, running[:, 2:3] - across, 0.0))


def keys_of(proj_ref, rows):
    return jnp.concatenate(
        [
            unit(proj_ref[rows, LANES : 2 * LANES]),
            unit(proj_ref[rows, 2 * LANES : 3 * LANES]),
        ],
        axis=0,
    )


def local_kernel(
    swap_ref, early_ref, late_ref, row_ref, state_ref, solved_ref, starts_ref, held_ref, proj_ref
):
    del swap_ref
    proj_ref[...] = early_ref[...] + late_ref[...]
    tokens = proj_ref.shape[0]
    width = LANES
    blocks = tokens // BLOCK
    span = 2 * BLOCK
    gates = proj_ref[:, 5 * width :]
    betas = 2.0 / (1.0 + jnp.exp(-(gates + row_ref[0:1, :])))
    runnings = running_decay(gates, row_ref)
    row_i = lax.broadcasted_iota(jnp.int32, (span, span), 0)
    col_i = lax.broadcasted_iota(jnp.int32, (span, span), 1)
    row_t, row_r = row_i % BLOCK, row_i // BLOCK
    col_t, col_r = col_i % BLOCK, col_i // BLOCK
    strict = (row_t > col_t) | ((row_t == col_t) & (row_r > col_r))
    within = (row_t == col_t) & (row_r > col_r)
    eye = jnp.where(row_i == col_i, 1.0, 0.0).astype(F32)
    visible = seen_before()
    levels = []
    size = 1
    while size < BLOCK:
        levels.append(
            (row_t // (2 * size) == col_t // (2 * size))
            & ((row_t // size) % 2 == 1)
            & ((col_t // size) % 2 == 0)
        )
        size *= 2

    def prepare(n):
        rows = slice(n * BLOCK, (n + 1) * BLOCK)
        keys = keys_of(proj_ref, rows)
        values = jnp.concatenate(
            [proj_ref[rows, 3 * width : 4 * width], proj_ref[rows, 4 * width : 5 * width]], axis=0
        )
        beta = jnp.concatenate([betas[rows, 0:1], betas[rows, 1:2]], axis=0)
        running = runnings[n]
        reach = reach_of(running, visible)
        keys_s = split(keys)
        scores = dot3(keys_s, keys_s, NT)
        system = jnp.where(strict, beta * jnp.concatenate([reach, reach], axis=0) * scores, 0.0)
        down = running[:, 2:3]
        grow = jnp.exp(down)
        grow2 = jnp.concatenate([grow, grow], axis=0)
        last = running[BLOCK - 1 : BLOCK, 2:3]
        tail = jnp.exp(last - down)
        return dict(
            keys=keys_s,
            system=system,
            right=jnp.concatenate([beta * grow2 * keys, beta * values], axis=1),
            tail=jnp.concatenate([tail, tail], axis=0),
            last=jnp.exp(last),
            inverse=eye - jnp.where(within, system, 0.0),
        )

    parts = [prepare(n) for n in range(blocks)]
    for level in levels:
        for part in parts:
            inverse = split(part["inverse"])
            corner = split(jnp.where(level, part["system"], 0.0))
            middle = dot3(corner, inverse, ROWS)
            part["inverse"] = part["inverse"] - dot3(inverse, split(middle), ROWS)
    for n, part in enumerate(parts):
        solved = dot3(split(part["inverse"]), split(part["right"]), ROWS)
        solved_ref[n] = solved
        part["step"] = dot3(split(solved * part["tail"]), part["keys"], TN)
    zero = jnp.zeros((width, width), F32)

    @pl.when(pl.program_id(0) == 0)
    def _():
        held_ref[:width, :] = eye
        held_ref[width:, :] = zero

    state = held_ref[...]
    for n, part in enumerate(parts):
        starts_ref[n] = state
        move = part["last"] * eye - part["step"][:width]
        state = dot3(split(state), split(move), ROWS)
        state = state + jnp.concatenate([zero, part["step"][width:]], axis=0)
    held_ref[...] = state
    state_ref[...] = state


def read_kernel(
    swap_ref, early_ref, late_ref, row_ref, solved_ref, starts_ref, query_ref, out_ref, proj_ref
):
    del swap_ref
    proj_ref[...] = early_ref[...] + late_ref[...]
    width = LANES
    visible = seen_before()
    runnings = running_decay(proj_ref[:, 5 * width :], row_ref)
    for n, running in enumerate(runnings):
        rows = slice(n * BLOCK, (n + 1) * BLOCK)
        query = unit(proj_ref[rows, 0:width])
        scores = dot3(split(query), split(keys_of(proj_ref, rows)), NT)
        attend = jnp.where(visible, reach_of(running, visible), 0.0) * scores
        seen = dot3(split(attend), split(solved_ref[n]), ROWS)
        query = query * jnp.exp(running[:, 2:3]) - seen[:, :width]
        reads = dot3(split(query), split(starts_ref[n]), NT)
        query_ref[rows, :] = reads[:, :width]
        out_ref[rows, :] = reads[:, width:] + seen[:, width:]


def local_pass(swap, proj, late, rows):
    tokens = proj.shape[0] // 2
    summed = pltpu.VMEM((tokens, proj.shape[1]), F32)
    blocks = tokens // BLOCK
    saved = jax.ShapeDtypeStruct((2 * blocks, 2 * LANES, LANES), F32)
    wide = jax.ShapeDtypeStruct((2 * blocks, LANES, 2 * LANES), F32)
    half = jax.ShapeDtypeStruct((proj.shape[0], LANES), F32)
    own_order = pl.BlockSpec((tokens, proj.shape[1]), lambda i, swap: (i ^ swap[0], 0))
    table = pl.BlockSpec(rows.shape, lambda i, swap: (0, 0))
    saved_spec = pl.BlockSpec((blocks, 2 * LANES, LANES), lambda i, swap: (i, 0, 0))
    wide_spec = pl.BlockSpec((blocks, LANES, 2 * LANES), lambda i, swap: (i, 0, 0))
    half_spec = pl.BlockSpec((tokens, LANES), lambda i, swap: (i, 0))
    window, solved, starts = pl.pallas_call(
        local_kernel,
        grid_spec=pltpu.PrefetchScalarGridSpec(
            num_scalar_prefetch=1,
            grid=(2,),
            in_specs=[own_order, own_order, table],
            out_specs=[
                pl.BlockSpec((2 * LANES, LANES), lambda i, swap: (0, 0)),
                wide_spec,
                saved_spec,
            ],
            scratch_shapes=[pltpu.VMEM((2 * LANES, LANES), F32), summed],
        ),
        out_shape=(jax.ShapeDtypeStruct((2 * LANES, LANES), F32), wide, saved),
        name="local",
    )(swap, proj, late, rows)
    queries, partial = pl.pallas_call(
        read_kernel,
        grid_spec=pltpu.PrefetchScalarGridSpec(
            num_scalar_prefetch=1,
            grid=(2,),
            in_specs=[own_order, own_order, table, wide_spec, saved_spec],
            out_specs=[half_spec, half_spec],
            scratch_shapes=[summed],
        ),
        out_shape=(half, half),
        name="reads",
    )(swap, proj, late, rows, solved, starts)
    return window, queries, partial


def finish_kernel(far_ref, near_ref, query_ref, part_ref, out_ref):
    near = near_ref[...]
    state = dot3(split(far_ref[...]), split(near[:LANES]), ROWS) + near[LANES:]
    total = part_ref[...] + dot3(split(query_ref[...]), split(state), NT)
    scale = jnp.sqrt(jnp.mean(total * total, axis=-1, keepdims=True) + 1e-06)
    out_ref[...] = (total / scale).astype(BF16)


def mix_kernel(rows_ref, weight_ref, out_ref):
    total = dot1(rows_ref[0], weight_ref[0], NT)
    for group in range(1, rows_ref.shape[0]):
        total = total + dot1(rows_ref[group], weight_ref[group], NT)
    out_ref[...] = total.astype(BF16)


def mix(rows, weights):
    groups, count, depth = rows.shape
    width = weights.shape[1]
    block = width // 4
    return pl.pallas_call(
        mix_kernel,
        grid=(width // block,),
        in_specs=[
            pl.BlockSpec((groups, count, depth), lambda i: (0, 0, 0)),
            pl.BlockSpec((groups, block, depth), lambda i: (0, i, 0)),
        ],
        out_specs=pl.BlockSpec((count, block), lambda i: (0, i)),
        out_shape=jax.ShapeDtypeStruct((count, width), BF16),
        name="mix",
    )(rows, weights)


def compose(before, now):
    moved = jnp.matmul(before, now[:LANES], precision=lax.Precision.HIGHEST)
    kept = lax.broadcasted_iota(jnp.int32, now.shape, 0) >= LANES
    return moved + jnp.where(kept, now, 0.0)[-before.shape[0] :]


def at(buffer, block, index):
    return lax.dynamic_update_slice_in_dim(buffer, block[None], index, axis=0)


def shards(tokens, w_proj, w_small, beta_bias, decay_rate, w_out):
    tok_rows, depth = tokens.shape
    ctx = lax.axis_index(CTX)
    count = lax.axis_size(CTX)
    z_size = count // Y_SIZE
    z, y = ctx // Y_SIZE, ctx % Y_SIZE
    pair, place = y // 2, y % 2
    second = (y + 1) // 2 % 2 == 1
    group = lax.axis_index("head")
    groups = lax.axis_size("head")
    rows_each = tok_rows // groups
    column, core = group // 2, group % 2
    columns = groups // 2

    flipped = lax.all_gather(w_out.T, ("head",) + CTX, axis=0, tiled=True)
    flipped = flipped.reshape(groups, w_out.shape[1] * count, w_out.shape[0])

    each = w_proj.shape[1] // 2
    gates = w_small.shape[1] // 2
    small = jnp.zeros((w_small.shape[0], LANES - gates), BF16)
    first_half = jnp.concatenate([w_proj[:, :each], w_small[:, :gates], small], axis=1)
    second_half = jnp.concatenate([w_proj[:, each:], w_small[:, gates:], small], axis=1)
    own = jnp.where(second, second_half, first_half)
    other = jnp.where(second, first_half, second_half)

    part = lax.dynamic_slice_in_dim(tokens, group * rows_each, rows_each, axis=0)
    part = permute(part, lambda z, y: (z, y ^ 1))
    quad = jnp.zeros((Y_SIZE,) + own.shape, BF16)
    quad = at(quad, own, y)
    for flip, block in ((3, own), (1, other), (2, other)):
        came = permute(block, lambda z, y, flip=flip: (z, y ^ flip))
        quad = at(quad, came, y ^ flip)
    quad = quad.reshape(Y_SIZE * own.shape[0], own.shape[1])
    weights = jnp.zeros((z_size,) + quad.shape, BF16)
    weights = at(weights, quad, z)
    parts = jnp.zeros((columns,) + part.shape, BF16)
    parts = at(parts, part, column)
    up = down = quad
    for step in range(1, z_size // 2):
        up = permute(up, lambda z, y: (z + 1, y))
        down = permute(down, lambda z, y: (z - 1, y))
        weights = at(weights, up, (z - step) % z_size)
        weights = at(weights, down, (z + step) % z_size)
    middle = quad.shape[0] // 2
    last = jnp.concatenate(
        [
            permute(up[:middle], lambda z, y: (z + 1, y)),
            permute(down[middle:], lambda z, y: (z - 1, y)),
        ],
        axis=0,
    )
    opposite = (z + z_size // 2) % z_size
    for step in range(1, columns):
        moved = permute_heads(part, lambda i, step=step: i + 2 * step)
        parts = at(parts, moved, (column - step) % columns)
    theirs = permute_heads(parts, lambda i: i ^ 1)
    even = jnp.where(core == 0, parts, theirs)
    odd = jnp.where(core == 0, theirs, parts)
    partner = jnp.stack([even, odd], axis=1).reshape(tok_rows, depth)
    both = jnp.concatenate([tokens, partner], axis=0)
    weights = weights.reshape(depth, quad.shape[1])
    projected = jnp.dot(both, weights, preferred_element_type=F32)
    behind = lax.dynamic_slice_in_dim(both, opposite * quad.shape[0], quad.shape[0], axis=1)
    late = jnp.dot(behind, last, preferred_element_type=F32)

    bias = jnp.where(second, beta_bias[1], beta_bias[0])
    rate = jnp.where(second, decay_rate[1:], decay_rate[:1])
    rows = jnp.stack(
        [
            jnp.pad(bias, (0, LANES - bias.shape[0])),
            jnp.pad(rate, (bias.shape[0], LANES - bias.shape[0] - 1)),
        ]
    )
    rows = jnp.pad(rows, ((0, 6), (0, 0)))
    window, queries, partial = local_pass(place.reshape(1), projected, late, rows)
    by = 1
    while 4 * by < count:
        before = shift(window, by)
        if by == 1:
            before, queries, partial = lax.optimization_barrier((before, queries, partial))
        window = compose(before, window)
        by *= 2
    near = shift(window, 1)
    far = shift(window[LANES:], by + 1)
    normed = pl.pallas_call(
        finish_kernel,
        out_shape=jax.ShapeDtypeStruct((2 * tok_rows, LANES), BF16),
        name="finish",
    )(far, near, queries, partial)
    stacked = normed.reshape(2 * groups, rows_each, LANES)
    taken = lax.all_to_all(stacked, ("p", "head"), split_axis=0, concat_axis=0, tiled=True)
    taken = taken.reshape(2, groups, rows_each, LANES)
    taken = jnp.where(pair == 0, taken, taken[::-1])
    taken = jnp.concatenate([taken[0], taken[1]], axis=2)
    return mix(taken, flipped)


def solution(mesh):
    sizes = dict(mesh.shape)
    finer = Mesh(
        mesh.devices.reshape(sizes["ctx"] // Y_SIZE, 2, 2, sizes["head"]), CTX + ("head",)
    )
    placed = (
        P(CTX, None),
        P(CTX, "head"),
        P(CTX, "head"),
        P("head", None),
        P("head"),
        P("head", CTX),
    )
    return jax.shard_map(
        shards, mesh=finer, in_specs=placed, out_specs=P(CTX + ("head",), None), check_vma=False
    )
```

```python
import jax
import jax.numpy as jnp
from jax import lax
from jax.experimental import pallas as pl
from jax.experimental.pallas import tpu as pltpu
from jax.sharding import Mesh
from jax.sharding import PartitionSpec as P

F32 = jnp.float32
BF16 = jnp.bfloat16
LANES = 128
BLOCK = 64
ROWS = (((1,), (0,)), ((), ()))
NT = (((1,), (1,)), ((), ()))
TN = (((0,), (0,)), ((), ()))


def split(array):
    high = array.astype(BF16)
    return high, (array - high.astype(F32)).astype(BF16)


def dot1(left, right, dims):
    return lax.dot_general(left, right, dims, preferred_element_type=F32)


def dot3(left, right, dims):
    (lc,), (rc,) = dims[0]
    kept = right[0].shape[1 - rc]
    lhs = jnp.concatenate(left, axis=lc)
    if kept == LANES:
        rhs = jnp.concatenate(right, axis=1 - rc)
        rhs = jnp.concatenate([rhs, rhs], axis=rc)
        out = dot1(lhs, rhs, dims)
        return out[:, :LANES] + out[:, LANES:]
    rhs = jnp.concatenate([right[0], right[0]], axis=rc)
    return dot1(lhs, rhs, dims) + dot1(left[0], right[1], dims)


Y_SIZE = 4
CTX = ("z", "m", "p")


def permute(array, move):
    count = lax.axis_size(CTX)
    z_size = count // Y_SIZE
    pairs = []
    for z in range(z_size):
        for y in range(Y_SIZE):
            to_z, to_y = move(z, y)
            pairs.append((z * Y_SIZE + y, (to_z % z_size) * Y_SIZE + to_y))
    return lax.ppermute(array, CTX, pairs)


def permute_heads(array, move):
    count = lax.axis_size("head")
    return lax.ppermute(array, "head", [(i, move(i) % count) for i in range(count)])


def shift(array, by):
    nodes = lax.axis_size(CTX) // 2

    def place(node, half):
        return node // 2 * Y_SIZE + ((0, 3), (1, 2))[half][node % 2]

    pairs = [(place(n, s), place(n + by, s)) for s in range(2) for n in range(nodes - by)]
    return lax.ppermute(array, CTX, pairs)


def unit(rows):
    return rows / jnp.sqrt(jnp.sum(rows * rows, axis=-1, keepdims=True) + 1e-06)


def running_decay(gates, row_ref):
    soft = jnp.maximum(gates, 0.0) + jnp.log1p(jnp.exp(-jnp.abs(gates)))
    log_decay = -row_ref[1:2, :] * soft
    row = lax.broadcasted_iota(jnp.int32, (BLOCK, BLOCK), 0)
    col = lax.broadcasted_iota(jnp.int32, (BLOCK, BLOCK), 1)
    lower = jnp.where(row >= col, 1.0, 0.0).astype(F32)
    return [
        jnp.dot(
            lower,
            log_decay[n * BLOCK : (n + 1) * BLOCK],
            precision=lax.Precision.HIGHEST,
            preferred_element_type=F32,
        )
        for n in range(gates.shape[0] // BLOCK)
    ]


def seen_before():
    return (
        lax.broadcasted_iota(jnp.int32, (BLOCK, 2 * BLOCK), 0)
        >= lax.broadcasted_iota(jnp.int32, (BLOCK, 2 * BLOCK), 1) % BLOCK
    )


def reach_of(running, visible):
    across = jnp.transpose(running)[2:3, :]
    across = jnp.concatenate([across, across], axis=1)
    return jnp.exp(jnp.where(visible, running[:, 2:3] - across, 0.0))


def keys_of(proj_ref, rows):
    return jnp.concatenate(
        [
            unit(proj_ref[rows, LANES : 2 * LANES]),
            unit(proj_ref[rows, 2 * LANES : 3 * LANES]),
        ],
        axis=0,
    )


def local_kernel(
    swap_ref, early_ref, behind_ref, last_ref, row_ref, state_ref, solved_ref, starts_ref, held_ref, proj_ref
):
    del swap_ref
    proj_ref[...] = early_ref[...] + dot1(behind_ref[...], last_ref[...], ROWS)
    tokens = proj_ref.shape[0]
    width = LANES
    blocks = tokens // BLOCK
    span = 2 * BLOCK
    gates = proj_ref[:, 5 * width :]
    betas = 2.0 / (1.0 + jnp.exp(-(gates + row_ref[0:1, :])))
    runnings = running_decay(gates, row_ref)
    row_i = lax.broadcasted_iota(jnp.int32, (span, span), 0)
    col_i = lax.broadcasted_iota(jnp.int32, (span, span), 1)
    row_t, row_r = row_i % BLOCK, row_i // BLOCK
    col_t, col_r = col_i % BLOCK, col_i // BLOCK
    strict = (row_t > col_t) | ((row_t == col_t) & (row_r > col_r))
    within = (row_t == col_t) & (row_r > col_r)
    eye = jnp.where(row_i == col_i, 1.0, 0.0).astype(F32)
    visible = seen_before()
    levels = []
    size = 1
    while size < BLOCK:
        levels.append(
            (row_t // (2 * size) == col_t // (2 * size))
            & ((row_t // size) % 2 == 1)
            & ((col_t // size) % 2 == 0)
        )
        size *= 2

    def prepare(n):
        rows = slice(n * BLOCK, (n + 1) * BLOCK)
        keys = keys_of(proj_ref, rows)
        values = jnp.concatenate(
            [proj_ref[rows, 3 * width : 4 * width], proj_ref[rows, 4 * width : 5 * width]], axis=0
        )
        beta = jnp.concatenate([betas[rows, 0:1], betas[rows, 1:2]], axis=0)
        running = runnings[n]
        reach = reach_of(running, visible)
        keys_s = split(keys)
        scores = dot3(keys_s, keys_s, NT)
        system = jnp.where(strict, beta * jnp.concatenate([reach, reach], axis=0) * scores, 0.0)
        down = running[:, 2:3]
        grow = jnp.exp(down)
        grow2 = jnp.concatenate([grow, grow], axis=0)
        last = running[BLOCK - 1 : BLOCK, 2:3]
        tail = jnp.exp(last - down)
        return dict(
            keys=keys_s,
            system=system,
            right=jnp.concatenate([beta * grow2 * keys, beta * values], axis=1),
            tail=jnp.concatenate([tail, tail], axis=0),
            last=jnp.exp(last),
            inverse=eye - jnp.where(within, system, 0.0),
        )

    parts = [prepare(n) for n in range(blocks)]
    for level in levels:
        for part in parts:
            inverse = split(part["inverse"])
            corner = split(jnp.where(level, part["system"], 0.0))
            middle = dot3(corner, inverse, ROWS)
            part["inverse"] = part["inverse"] - dot3(inverse, split(middle), ROWS)
    for n, part in enumerate(parts):
        solved = dot3(split(part["inverse"]), split(part["right"]), ROWS)
        solved_ref[n] = solved
        part["step"] = dot3(split(solved * part["tail"]), part["keys"], TN)
    zero = jnp.zeros((width, width), F32)

    @pl.when(pl.program_id(0) == 0)
    def _():
        held_ref[:width, :] = eye
        held_ref[width:, :] = zero

    state = held_ref[...]
    for n, part in enumerate(parts):
        starts_ref[n] = state
        move = part["last"] * eye - part["step"][:width]
        state = dot3(split(state), split(move), ROWS)
        state = state + jnp.concatenate([zero, part["step"][width:]], axis=0)
    held_ref[...] = state
    state_ref[...] = state


def read_kernel(
    swap_ref, early_ref, behind_ref, last_ref, row_ref, solved_ref, starts_ref, query_ref, out_ref, proj_ref
):
    del swap_ref
    proj_ref[...] = early_ref[...] + dot1(behind_ref[...], last_ref[...], ROWS)
    width = LANES
    visible = seen_before()
    runnings = running_decay(proj_ref[:, 5 * width :], row_ref)
    for n, running in enumerate(runnings):
        rows = slice(n * BLOCK, (n + 1) * BLOCK)
        query = unit(proj_ref[rows, 0:width])
        scores = dot3(split(query), split(keys_of(proj_ref, rows)), NT)
        attend = jnp.where(visible, reach_of(running, visible), 0.0) * scores
        seen = dot3(split(attend), split(solved_ref[n]), ROWS)
        query = query * jnp.exp(running[:, 2:3]) - seen[:, :width]
        reads = dot3(split(query), split(starts_ref[n]), NT)
        query_ref[rows, :] = reads[:, :width]
        out_ref[rows, :] = reads[:, width:] + seen[:, width:]


def local_pass(swap, proj, behind, last, rows):
    tokens = proj.shape[0] // 2
    summed = pltpu.VMEM((tokens, proj.shape[1]), F32)
    blocks = tokens // BLOCK
    saved = jax.ShapeDtypeStruct((2 * blocks, 2 * LANES, LANES), F32)
    wide = jax.ShapeDtypeStruct((2 * blocks, LANES, 2 * LANES), F32)
    half = jax.ShapeDtypeStruct((proj.shape[0], LANES), F32)
    own_order = pl.BlockSpec((tokens, proj.shape[1]), lambda i, swap: (i ^ swap[0], 0))
    own_behind = pl.BlockSpec((tokens, behind.shape[1]), lambda i, swap: (i ^ swap[0], 0))
    whole = pl.BlockSpec(last.shape, lambda i, swap: (0, 0))
    table = pl.BlockSpec(rows.shape, lambda i, swap: (0, 0))
    saved_spec = pl.BlockSpec((blocks, 2 * LANES, LANES), lambda i, swap: (i, 0, 0))
    wide_spec = pl.BlockSpec((blocks, LANES, 2 * LANES), lambda i, swap: (i, 0, 0))
    half_spec = pl.BlockSpec((tokens, LANES), lambda i, swap: (i, 0))
    window, solved, starts = pl.pallas_call(
        local_kernel,
        grid_spec=pltpu.PrefetchScalarGridSpec(
            num_scalar_prefetch=1,
            grid=(2,),
            in_specs=[own_order, own_behind, whole, table],
            out_specs=[
                pl.BlockSpec((2 * LANES, LANES), lambda i, swap: (0, 0)),
                wide_spec,
                saved_spec,
            ],
            scratch_shapes=[pltpu.VMEM((2 * LANES, LANES), F32), summed],
        ),
        out_shape=(jax.ShapeDtypeStruct((2 * LANES, LANES), F32), wide, saved),
        name="local",
    )(swap, proj, behind, last, rows)
    queries, partial = pl.pallas_call(
        read_kernel,
        grid_spec=pltpu.PrefetchScalarGridSpec(
            num_scalar_prefetch=1,
            grid=(2,),
            in_specs=[own_order, own_behind, whole, table, wide_spec, saved_spec],
            out_specs=[half_spec, half_spec],
            scratch_shapes=[summed],
        ),
        out_shape=(half, half),
        name="reads",
    )(swap, proj, behind, last, rows, solved, starts)
    return window, queries, partial


def finish_kernel(far_ref, near_ref, query_ref, part_ref, out_ref):
    near = near_ref[...]
    state = dot3(split(far_ref[...]), split(near[:LANES]), ROWS) + near[LANES:]
    total = part_ref[...] + dot3(split(query_ref[...]), split(state), NT)
    scale = jnp.sqrt(jnp.mean(total * total, axis=-1, keepdims=True) + 1e-06)
    out_ref[...] = (total / scale).astype(BF16)


def mix_kernel(rows_ref, weight_ref, out_ref):
    total = dot1(rows_ref[0], weight_ref[0], NT)
    for group in range(1, rows_ref.shape[0]):
        total = total + dot1(rows_ref[group], weight_ref[group], NT)
    out_ref[...] = total.astype(BF16)


def mix(rows, weights):
    groups, count, depth = rows.shape
    width = weights.shape[1]
    block = width // 4
    return pl.pallas_call(
        mix_kernel,
        grid=(width // block,),
        in_specs=[
            pl.BlockSpec((groups, count, depth), lambda i: (0, 0, 0)),
            pl.BlockSpec((groups, block, depth), lambda i: (0, i, 0)),
        ],
        out_specs=pl.BlockSpec((count, block), lambda i: (0, i)),
        out_shape=jax.ShapeDtypeStruct((count, width), BF16),
        name="mix",
    )(rows, weights)


def compose(before, now):
    moved = jnp.matmul(before, now[:LANES], precision=lax.Precision.HIGHEST)
    kept = lax.broadcasted_iota(jnp.int32, now.shape, 0) >= LANES
    return moved + jnp.where(kept, now, 0.0)[-before.shape[0] :]


def at(buffer, block, index):
    return lax.dynamic_update_slice_in_dim(buffer, block[None], index, axis=0)


def shards(tokens, w_proj, w_small, beta_bias, decay_rate, w_out):
    tok_rows, depth = tokens.shape
    ctx = lax.axis_index(CTX)
    count = lax.axis_size(CTX)
    z_size = count // Y_SIZE
    z, y = ctx // Y_SIZE, ctx % Y_SIZE
    pair, place = y // 2, y % 2
    second = (y + 1) // 2 % 2 == 1
    group = lax.axis_index("head")
    groups = lax.axis_size("head")
    rows_each = tok_rows // groups
    column, core = group // 2, group % 2
    columns = groups // 2

    flipped = lax.all_gather(w_out.T, ("head",) + CTX, axis=0, tiled=True)
    flipped = flipped.reshape(groups, w_out.shape[1] * count, w_out.shape[0])

    each = w_proj.shape[1] // 2
    gates = w_small.shape[1] // 2
    small = jnp.zeros((w_small.shape[0], LANES - gates), BF16)
    first_half = jnp.concatenate([w_proj[:, :each], w_small[:, :gates], small], axis=1)
    second_half = jnp.concatenate([w_proj[:, each:], w_small[:, gates:], small], axis=1)
    own = jnp.where(second, second_half, first_half)
    other = jnp.where(second, first_half, second_half)

    part = lax.dynamic_slice_in_dim(tokens, group * rows_each, rows_each, axis=0)
    part = permute(part, lambda z, y: (z, y ^ 1))
    quad = jnp.zeros((Y_SIZE,) + own.shape, BF16)
    quad = at(quad, own, y)
    for flip, block in ((3, own), (1, other), (2, other)):
        came = permute(block, lambda z, y, flip=flip: (z, y ^ flip))
        quad = at(quad, came, y ^ flip)
    quad = quad.reshape(Y_SIZE * own.shape[0], own.shape[1])
    weights = jnp.zeros((z_size,) + quad.shape, BF16)
    weights = at(weights, quad, z)
    parts = jnp.zeros((columns,) + part.shape, BF16)
    parts = at(parts, part, column)
    up = down = quad
    for step in range(1, z_size // 2):
        up = permute(up, lambda z, y: (z + 1, y))
        down = permute(down, lambda z, y: (z - 1, y))
        weights = at(weights, up, (z - step) % z_size)
        weights = at(weights, down, (z + step) % z_size)
    for step in range(1, columns):
        moved = permute_heads(part, lambda i, step=step: i + 2 * step)
        parts = at(parts, moved, (column - step) % columns)
    theirs = permute_heads(parts, lambda i: i ^ 1)
    up, down, theirs = lax.optimization_barrier((up, down, theirs))
    middle = quad.shape[0] // 2
    last = jnp.concatenate(
        [
            permute(up[:middle], lambda z, y: (z + 1, y)),
            permute(down[middle:], lambda z, y: (z - 1, y)),
        ],
        axis=0,
    )
    opposite = (z + z_size // 2) % z_size
    even = jnp.where(core == 0, parts, theirs)
    odd = jnp.where(core == 0, theirs, parts)
    partner = jnp.stack([even, odd], axis=1).reshape(tok_rows, depth)
    both = jnp.concatenate([tokens, partner], axis=0)
    weights = weights.reshape(depth, quad.shape[1])
    projected = jnp.dot(both, weights, preferred_element_type=F32)
    behind = lax.dynamic_slice_in_dim(both, opposite * quad.shape[0], quad.shape[0], axis=1)

    bias = jnp.where(second, beta_bias[1], beta_bias[0])
    rate = jnp.where(second, decay_rate[1:], decay_rate[:1])
    rows = jnp.stack(
        [
            jnp.pad(bias, (0, LANES - bias.shape[0])),
            jnp.pad(rate, (bias.shape[0], LANES - bias.shape[0] - 1)),
        ]
    )
    rows = jnp.pad(rows, ((0, 6), (0, 0)))
    window, queries, partial = local_pass(place.reshape(1), projected, behind, last, rows)
    by = 1
    while 4 * by < count:
        before = shift(window, by)
        if by == 1:
            before, queries, partial = lax.optimization_barrier((before, queries, partial))
        window = compose(before, window)
        by *= 2
    near = shift(window, 1)
    far = shift(window[LANES:], by + 1)
    normed = pl.pallas_call(
        finish_kernel,
        out_shape=jax.ShapeDtypeStruct((2 * tok_rows, LANES), BF16),
        name="finish",
    )(far, near, queries, partial)
    stacked = normed.reshape(2 * groups, rows_each, LANES)
    taken = lax.all_to_all(stacked, ("p", "head"), split_axis=0, concat_axis=0, tiled=True)
    taken = taken.reshape(2, groups, rows_each, LANES)
    taken = jnp.where(pair == 0, taken, taken[::-1])
    taken = jnp.concatenate([taken[0], taken[1]], axis=2)
    return mix(taken, flipped)


def solution(mesh):
    sizes = dict(mesh.shape)
    finer = Mesh(
        mesh.devices.reshape(sizes["ctx"] // Y_SIZE, 2, 2, sizes["head"]), CTX + ("head",)
    )
    placed = (
        P(CTX, None),
        P(CTX, "head"),
        P(CTX, "head"),
        P("head", None),
        P("head"),
        P("head", CTX),
    )
    return jax.shard_map(
        shards, mesh=finer, in_specs=placed, out_specs=P(CTX + ("head",), None), check_vma=False
    )
```

```python
import jax
import jax.numpy as jnp
from jax import lax
from jax.experimental import pallas as pl
from jax.experimental.pallas import tpu as pltpu
from jax.sharding import Mesh
from jax.sharding import PartitionSpec as P

F32 = jnp.float32
BF16 = jnp.bfloat16
LANES = 128
BLOCK = 64
ROWS = (((1,), (0,)), ((), ()))
NT = (((1,), (1,)), ((), ()))
TN = (((0,), (0,)), ((), ()))


def split(array):
    high = array.astype(BF16)
    return high, (array - high.astype(F32)).astype(BF16)


def dot1(left, right, dims):
    return lax.dot_general(left, right, dims, preferred_element_type=F32)


def dot3(left, right, dims):
    (lc,), (rc,) = dims[0]
    kept = right[0].shape[1 - rc]
    lhs = jnp.concatenate(left, axis=lc)
    if kept == LANES:
        rhs = jnp.concatenate(right, axis=1 - rc)
        rhs = jnp.concatenate([rhs, rhs], axis=rc)
        out = dot1(lhs, rhs, dims)
        return out[:, :LANES] + out[:, LANES:]
    rhs = jnp.concatenate([right[0], right[0]], axis=rc)
    return dot1(lhs, rhs, dims) + dot1(left[0], right[1], dims)


Y_SIZE = 4
CTX = ("z", "m", "p")


def permute(array, move):
    count = lax.axis_size(CTX)
    z_size = count // Y_SIZE
    pairs = []
    for z in range(z_size):
        for y in range(Y_SIZE):
            to_z, to_y = move(z, y)
            pairs.append((z * Y_SIZE + y, (to_z % z_size) * Y_SIZE + to_y))
    return lax.ppermute(array, CTX, pairs)


def permute_heads(array, move):
    count = lax.axis_size("head")
    return lax.ppermute(array, "head", [(i, move(i) % count) for i in range(count)])


def shift(array, by):
    nodes = lax.axis_size(CTX) // 2

    def place(node, half):
        return node // 2 * Y_SIZE + ((0, 3), (1, 2))[half][node % 2]

    pairs = [(place(n, s), place(n + by, s)) for s in range(2) for n in range(nodes - by)]
    return lax.ppermute(array, CTX, pairs)


def unit(rows):
    return rows / jnp.sqrt(jnp.sum(rows * rows, axis=-1, keepdims=True) + 1e-06)


def running_decay(gates, row_ref):
    soft = jnp.maximum(gates, 0.0) + jnp.log1p(jnp.exp(-jnp.abs(gates)))
    log_decay = -row_ref[1:2, :] * soft
    row = lax.broadcasted_iota(jnp.int32, (BLOCK, BLOCK), 0)
    col = lax.broadcasted_iota(jnp.int32, (BLOCK, BLOCK), 1)
    lower = jnp.where(row >= col, 1.0, 0.0).astype(F32)
    return [
        jnp.dot(
            lower,
            log_decay[n * BLOCK : (n + 1) * BLOCK],
            precision=lax.Precision.HIGHEST,
            preferred_element_type=F32,
        )
        for n in range(gates.shape[0] // BLOCK)
    ]


def seen_before():
    return (
        lax.broadcasted_iota(jnp.int32, (BLOCK, 2 * BLOCK), 0)
        >= lax.broadcasted_iota(jnp.int32, (BLOCK, 2 * BLOCK), 1) % BLOCK
    )


def reach_of(running, visible):
    across = jnp.transpose(running)[2:3, :]
    across = jnp.concatenate([across, across], axis=1)
    return jnp.exp(jnp.where(visible, running[:, 2:3] - across, 0.0))


def keys_of(proj_ref, rows):
    return jnp.concatenate(
        [
            unit(proj_ref[rows, LANES : 2 * LANES]),
            unit(proj_ref[rows, 2 * LANES : 3 * LANES]),
        ],
        axis=0,
    )


def local_kernel(
    swap_ref, early_ref, behind_ref, last_ref, row_ref, state_ref, solved_ref, starts_ref, held_ref, proj_ref
):
    del swap_ref
    proj_ref[...] = early_ref[...] + dot1(behind_ref[...], last_ref[...], ROWS)
    tokens = proj_ref.shape[0]
    width = LANES
    blocks = tokens // BLOCK
    span = 2 * BLOCK
    gates = proj_ref[:, 5 * width :]
    betas = 2.0 / (1.0 + jnp.exp(-(gates + row_ref[0:1, :])))
    runnings = running_decay(gates, row_ref)
    row_i = lax.broadcasted_iota(jnp.int32, (span, span), 0)
    col_i = lax.broadcasted_iota(jnp.int32, (span, span), 1)
    row_t, row_r = row_i % BLOCK, row_i // BLOCK
    col_t, col_r = col_i % BLOCK, col_i // BLOCK
    strict = (row_t > col_t) | ((row_t == col_t) & (row_r > col_r))
    within = (row_t == col_t) & (row_r > col_r)
    eye = jnp.where(row_i == col_i, 1.0, 0.0).astype(F32)
    visible = seen_before()
    levels = []
    size = 1
    while size < BLOCK:
        levels.append(
            (row_t // (2 * size) == col_t // (2 * size))
            & ((row_t // size) % 2 == 1)
            & ((col_t // size) % 2 == 0)
        )
        size *= 2

    def prepare(n):
        rows = slice(n * BLOCK, (n + 1) * BLOCK)
        keys = keys_of(proj_ref, rows)
        values = jnp.concatenate(
            [proj_ref[rows, 3 * width : 4 * width], proj_ref[rows, 4 * width : 5 * width]], axis=0
        )
        beta = jnp.concatenate([betas[rows, 0:1], betas[rows, 1:2]], axis=0)
        running = runnings[n]
        reach = reach_of(running, visible)
        keys_s = split(keys)
        scores = dot3(keys_s, keys_s, NT)
        system = jnp.where(strict, beta * jnp.concatenate([reach, reach], axis=0) * scores, 0.0)
        down = running[:, 2:3]
        grow = jnp.exp(down)
        grow2 = jnp.concatenate([grow, grow], axis=0)
        last = running[BLOCK - 1 : BLOCK, 2:3]
        tail = jnp.exp(last - down)
        return dict(
            keys=keys_s,
            system=system,
            right=jnp.concatenate([beta * grow2 * keys, beta * values], axis=1),
            tail=jnp.concatenate([tail, tail], axis=0),
            last=jnp.exp(last),
            inverse=eye - jnp.where(within, system, 0.0),
        )

    parts = [prepare(n) for n in range(blocks)]
    for level in levels:
        for part in parts:
            inverse = split(part["inverse"])
            corner = split(jnp.where(level, part["system"], 0.0))
            middle = dot3(corner, inverse, ROWS)
            part["inverse"] = part["inverse"] - dot3(inverse, split(middle), ROWS)
    for n, part in enumerate(parts):
        solved = dot3(split(part["inverse"]), split(part["right"]), ROWS)
        solved_ref[n] = solved
        part["step"] = dot3(split(solved * part["tail"]), part["keys"], TN)
    zero = jnp.zeros((width, width), F32)

    @pl.when(pl.program_id(0) == 0)
    def _():
        held_ref[:width, :] = eye
        held_ref[width:, :] = zero

    state = held_ref[...]
    for n, part in enumerate(parts):
        starts_ref[n] = state
        move = part["last"] * eye - part["step"][:width]
        state = dot3(split(state), split(move), ROWS)
        state = state + jnp.concatenate([zero, part["step"][width:]], axis=0)
    held_ref[...] = state
    state_ref[...] = state


def read_kernel(
    swap_ref, early_ref, behind_ref, last_ref, row_ref, solved_ref, starts_ref, query_ref, out_ref, proj_ref
):
    del swap_ref
    proj_ref[...] = early_ref[...] + dot1(behind_ref[...], last_ref[...], ROWS)
    width = LANES
    visible = seen_before()
    runnings = running_decay(proj_ref[:, 5 * width :], row_ref)
    for n, running in enumerate(runnings):
        rows = slice(n * BLOCK, (n + 1) * BLOCK)
        query = unit(proj_ref[rows, 0:width])
        scores = dot3(split(query), split(keys_of(proj_ref, rows)), NT)
        attend = jnp.where(visible, reach_of(running, visible), 0.0) * scores
        seen = dot3(split(attend), split(solved_ref[n]), ROWS)
        query = query * jnp.exp(running[:, 2:3]) - seen[:, :width]
        reads = dot3(split(query), split(starts_ref[n]), NT)
        query_ref[rows, :] = reads[:, :width]
        out_ref[rows, :] = reads[:, width:] + seen[:, width:]


def local_pass(swap, proj, behind, last, rows):
    tokens = proj.shape[0] // 2
    summed = pltpu.VMEM((tokens, proj.shape[1]), F32)
    blocks = tokens // BLOCK
    saved = jax.ShapeDtypeStruct((2 * blocks, 2 * LANES, LANES), F32)
    wide = jax.ShapeDtypeStruct((2 * blocks, LANES, 2 * LANES), F32)
    half = jax.ShapeDtypeStruct((proj.shape[0], LANES), F32)
    own_order = pl.BlockSpec((tokens, proj.shape[1]), lambda i, swap: (i ^ swap[0], 0))
    own_behind = pl.BlockSpec((tokens, behind.shape[1]), lambda i, swap: (i ^ swap[0], 0))
    whole = pl.BlockSpec(last.shape, lambda i, swap: (0, 0))
    table = pl.BlockSpec(rows.shape, lambda i, swap: (0, 0))
    saved_spec = pl.BlockSpec((blocks, 2 * LANES, LANES), lambda i, swap: (i, 0, 0))
    wide_spec = pl.BlockSpec((blocks, LANES, 2 * LANES), lambda i, swap: (i, 0, 0))
    half_spec = pl.BlockSpec((tokens, LANES), lambda i, swap: (i, 0))
    window, solved, starts = pl.pallas_call(
        local_kernel,
        grid_spec=pltpu.PrefetchScalarGridSpec(
            num_scalar_prefetch=1,
            grid=(2,),
            in_specs=[own_order, own_behind, whole, table],
            out_specs=[
                pl.BlockSpec((2 * LANES, LANES), lambda i, swap: (0, 0)),
                wide_spec,
                saved_spec,
            ],
            scratch_shapes=[pltpu.VMEM((2 * LANES, LANES), F32), summed],
        ),
        out_shape=(jax.ShapeDtypeStruct((2 * LANES, LANES), F32), wide, saved),
        name="local",
    )(swap, proj, behind, last, rows)
    queries, partial = pl.pallas_call(
        read_kernel,
        grid_spec=pltpu.PrefetchScalarGridSpec(
            num_scalar_prefetch=1,
            grid=(2,),
            in_specs=[own_order, own_behind, whole, table, wide_spec, saved_spec],
            out_specs=[half_spec, half_spec],
            scratch_shapes=[summed],
        ),
        out_shape=(half, half),
        name="reads",
    )(swap, proj, behind, last, rows, solved, starts)
    return window, queries, partial


def finish_kernel(far_ref, near_ref, query_ref, part_ref, out_ref):
    near = near_ref[...]
    state = dot3(split(far_ref[...]), split(near[:LANES]), ROWS) + near[LANES:]
    total = part_ref[...] + dot3(split(query_ref[...]), split(state), NT)
    scale = jnp.sqrt(jnp.mean(total * total, axis=-1, keepdims=True) + 1e-06)
    out_ref[...] = (total / scale).astype(BF16)


def mix_kernel(first_ref, rows_ref, weight_ref, out_ref):
    first = first_ref[0]
    total = 0.0
    for group in range(rows_ref.shape[1]):
        rows = jnp.concatenate([rows_ref[first, group], rows_ref[1 - first, group]], axis=1)
        total = total + dot1(rows, weight_ref[group], NT)
    out_ref[...] = total.astype(BF16)


def mix(first, rows, weights):
    count = rows.shape[2]
    groups, width, depth = weights.shape
    block = width // 4
    return pl.pallas_call(
        mix_kernel,
        grid_spec=pltpu.PrefetchScalarGridSpec(
            num_scalar_prefetch=1,
            grid=(width // block,),
            in_specs=[
                pl.BlockSpec(rows.shape, lambda i, first: (0, 0, 0, 0)),
                pl.BlockSpec((groups, block, depth), lambda i, first: (0, i, 0)),
            ],
            out_specs=pl.BlockSpec((count, block), lambda i, first: (0, i)),
        ),
        out_shape=jax.ShapeDtypeStruct((count, width), BF16),
        name="mix",
    )(first, rows, weights)


def compose(before, now):
    moved = jnp.matmul(before, now[:LANES], precision=lax.Precision.HIGHEST)
    kept = lax.broadcasted_iota(jnp.int32, now.shape, 0) >= LANES
    return moved + jnp.where(kept, now, 0.0)[-before.shape[0] :]


def at(buffer, block, index):
    return lax.dynamic_update_slice_in_dim(buffer, block[None], index, axis=0)


def shards(tokens, w_proj, w_small, beta_bias, decay_rate, w_out):
    tok_rows, depth = tokens.shape
    ctx = lax.axis_index(CTX)
    count = lax.axis_size(CTX)
    z_size = count // Y_SIZE
    z, y = ctx // Y_SIZE, ctx % Y_SIZE
    pair, place = y // 2, y % 2
    second = (y + 1) // 2 % 2 == 1
    group = lax.axis_index("head")
    groups = lax.axis_size("head")
    rows_each = tok_rows // groups
    column, core = group // 2, group % 2
    columns = groups // 2

    flipped = lax.all_gather(w_out.T, ("head",) + CTX, axis=0, tiled=True)
    flipped = flipped.reshape(groups, w_out.shape[1] * count, w_out.shape[0])

    each = w_proj.shape[1] // 2
    gates = w_small.shape[1] // 2
    small = jnp.zeros((w_small.shape[0], LANES - gates), BF16)
    first_half = jnp.concatenate([w_proj[:, :each], w_small[:, :gates], small], axis=1)
    second_half = jnp.concatenate([w_proj[:, each:], w_small[:, gates:], small], axis=1)
    own = jnp.where(second, second_half, first_half)
    other = jnp.where(second, first_half, second_half)

    part = lax.dynamic_slice_in_dim(tokens, group * rows_each, rows_each, axis=0)
    part = permute(part, lambda z, y: (z, y ^ 1))
    quad = jnp.zeros((Y_SIZE,) + own.shape, BF16)
    quad = at(quad, own, y)
    for flip, block in ((3, own), (1, other), (2, other)):
        came = permute(block, lambda z, y, flip=flip: (z, y ^ flip))
        quad = at(quad, came, y ^ flip)
    quad = quad.reshape(Y_SIZE * own.shape[0], own.shape[1])
    weights = jnp.zeros((z_size,) + quad.shape, BF16)
    weights = at(weights, quad, z)
    parts = jnp.zeros((columns,) + part.shape, BF16)
    parts = at(parts, part, column)
    up = down = quad
    for step in range(1, z_size // 2):
        up = permute(up, lambda z, y: (z + 1, y))
        down = permute(down, lambda z, y: (z - 1, y))
        weights = at(weights, up, (z - step) % z_size)
        weights = at(weights, down, (z + step) % z_size)
    for step in range(1, columns):
        moved = permute_heads(part, lambda i, step=step: i + 2 * step)
        parts = at(parts, moved, (column - step) % columns)
    theirs = permute_heads(parts, lambda i: i ^ 1)
    up, down, theirs = lax.optimization_barrier((up, down, theirs))
    middle = quad.shape[0] // 2
    last = jnp.concatenate(
        [
            permute(up[:middle], lambda z, y: (z + 1, y)),
            permute(down[middle:], lambda z, y: (z - 1, y)),
        ],
        axis=0,
    )
    opposite = (z + z_size // 2) % z_size
    even = jnp.where(core == 0, parts, theirs)
    odd = jnp.where(core == 0, theirs, parts)
    partner = jnp.stack([even, odd], axis=1).reshape(tok_rows, depth)
    both = jnp.concatenate([tokens, partner], axis=0)
    weights = weights.reshape(depth, quad.shape[1])
    projected = jnp.dot(both, weights, preferred_element_type=F32)
    behind = lax.dynamic_slice_in_dim(both, opposite * quad.shape[0], quad.shape[0], axis=1)

    bias = jnp.where(second, beta_bias[1], beta_bias[0])
    rate = jnp.where(second, decay_rate[1:], decay_rate[:1])
    rows = jnp.stack(
        [
            jnp.pad(bias, (0, LANES - bias.shape[0])),
            jnp.pad(rate, (bias.shape[0], LANES - bias.shape[0] - 1)),
        ]
    )
    rows = jnp.pad(rows, ((0, 6), (0, 0)))
    window, queries, partial = local_pass(place.reshape(1), projected, behind, last, rows)
    by = 1
    while 4 * by < count:
        before = shift(window, by)
        if by == 1:
            before, queries, partial = lax.optimization_barrier((before, queries, partial))
        window = compose(before, window)
        by *= 2
    near = shift(window, 1)
    far = shift(window[LANES:], by + 1)
    normed = pl.pallas_call(
        finish_kernel,
        out_shape=jax.ShapeDtypeStruct((2 * tok_rows, LANES), BF16),
        name="finish",
    )(far, near, queries, partial)
    stacked = normed.reshape(2 * groups, rows_each, LANES)
    taken = lax.all_to_all(stacked, ("p", "head"), split_axis=0, concat_axis=0, tiled=True)
    taken = taken.reshape(2, groups, rows_each, LANES)
    return mix(pair.reshape(1), taken, flipped)


def solution(mesh):
    sizes = dict(mesh.shape)
    finer = Mesh(
        mesh.devices.reshape(sizes["ctx"] // Y_SIZE, 2, 2, sizes["head"]), CTX + ("head",)
    )
    placed = (
        P(CTX, None),
        P(CTX, "head"),
        P(CTX, "head"),
        P("head", None),
        P("head"),
        P("head", CTX),
    )
    return jax.shard_map(
        shards, mesh=finer, in_specs=placed, out_specs=P(CTX + ("head",), None), check_vma=False
    )
```
